256 devices in a mesh: dp: 64 (over y, x, z_lo), mp: 4 (over z_hi, core).
Axes of the slice: x: 4, y: 4, z: 8 (z_hi: 2, z_lo: 4; z = z_hi * 4 + z_lo), core: 2. Of those that a mesh axis runs over, the one named last changes fastest.
Arguments:
- act_in: bfloat16 [8192, 4096], P('dp', 'mp'), may hold values from -6 to 6
- grad_in: bfloat16 [8192, 16384], P('dp'), may hold values from -6 to 6
- query_act: bfloat16 [1024, 4096], P('dp', 'mp'), may hold values from -6 to 6
- query_grad: bfloat16 [1024, 16384], P('dp'), may hold values from -6 to 6
- act_basis: bfloat16 [4096, 128], P('mp'), may hold values from -1.1 to 1.1
- grad_basis: bfloat16 [16384, 128], P('dp'), may hold values from -1.1 to 1.1
- seq_lengths: int32 [4], replicated, may hold values from 1 to 2048, 6144 in all
Outputs:
- moments: float32 [4096, 16384], P('mp', 'dp')
- scores: float32 [64, 4], replicated
The draws below stay inside these ranges and needn't reach their ends.
Inputs may be any that keep to these rules, and one draw needn't show every extreme that they name: `seq_lengths`: live tokens are the first ones of each sequence, and one sequence is full.
All inputs are finite; a program needn't handle non-finite values.
Results may differ from the reference program's by a relative error of at most 0.0046.
Values may be sent and summed in bfloat16 or wider, within the bound.
No kernel may reach another device: no remote copies, remote signals or barrier semaphores. Data moves between devices by JAX's collectives and lax.ppermute only.
A program may use at most 192 MiB of HBM per device.

```python
import math
import jax
import jax.numpy as jnp
import numpy as np
from jax import lax

D = 4096
FF = 16384
BLOCK = 128
SEQS = 4
QUERIES = 64
QUERY_LEN = 16
TOKENS = 8192
SEQ_LEN = 2048
QROWS = 1024


def basis_blocks(key, total_rows):
    first_key, second_key = jax.random.split(key)
    base = jnp.clip(jax.random.normal(first_key, (total_rows, BLOCK), jnp.float32), -4.0, 4.0)
    column_scale = jnp.exp(jax.random.uniform(second_key, (total_rows // BLOCK, 1, BLOCK), jnp.float32, math.log(0.3), math.log(3.0)))
    blocks = base.reshape(total_rows // BLOCK, BLOCK, BLOCK) * column_scale / math.sqrt(BLOCK)
    blocks = jnp.clip(blocks, -1.09375, 1.09375)
    return blocks.reshape(total_rows, BLOCK).astype(jnp.bfloat16)


def draw_act_basis(key, part):
    return basis_blocks(jax.random.fold_in(key, 11), D)


def draw_grad_basis(key, part):
    return basis_blocks(jax.random.fold_in(key, 23), FF)


def level_of(key, shape, cuts, smallest, top_value):
    factor_of = 1.0
    for dim, blocks in cuts:
        steps = jax.random.uniform(jax.random.fold_in(jax.random.fold_in(key, 6), dim), (blocks,), jnp.float32, smallest / len(cuts), top_value / len(cuts))
        factor_of = factor_of * jnp.repeat(jnp.exp(steps), shape[dim] // blocks).reshape((-1,) + (1,) * (len(shape) - 1 - dim))
    return factor_of


def split_up(number_of, total, limit, skew):
    portions = [(1 << 20) // math.isqrt(rank ** skew) + 1 for rank in range(2, number_of + 1)]
    spare, given = total - limit - (number_of - 1), [1] * (number_of - 1)
    while spare > 0:
        movable = [i for i in range(number_of - 1) if given[i] < limit]
        whole, remaining = sum([portions[i] for i in movable]), spare
        for i in movable:
            more = min(limit - given[i], max(1, remaining * portions[i] // whole), spare)
            given[i] = given[i] + more
            spare = spare - more
    return np.array([limit] + given)


def uneven(stream_key, amount, total, reach, slope):
    if amount == 2:
        one = jax.random.randint(stream_key, (), max(1, total - reach), min(reach, total - 1) + 1)
        return jnp.stack([one, total - one])
    sizes = jnp.asarray(split_up(amount, total, reach, slope), jnp.int32)
    pairs = (amount - 1) // 2
    donor, sink = sizes[1:1 + 2 * pairs:2], sizes[2:2 + 2 * pairs:2]
    margin = jnp.minimum(donor - 1, reach - sink)
    shifted = jax.random.randint(jax.random.fold_in(stream_key, 1), (pairs,), 0, 1 << 20) % (margin + 1)
    sizes = sizes.at[1:1 + 2 * pairs:2].set(donor - shifted).at[2:2 + 2 * pairs:2].set(sink + shifted)
    return sizes[jax.random.permutation(jax.random.fold_in(stream_key, 2), amount)]


def bell_draw(own_key, shape, width, limit, cuts=(), kind=jnp.bfloat16):
    entries = width * jax.random.normal(own_key, shape, jnp.float32)
    if cuts:
        entries = entries * level_of(own_key, shape, cuts, -0.22, 0.18)
    return jnp.clip(entries, -limit, limit).astype(kind)


def setup_inputs(seed: int = 0) -> dict:
    seeds = jax.random.split(jax.random.key(seed), 8)
    return {
        "act_in": bell_draw(seeds[0], (TOKENS, D), 1.0, 6.0, ((0, 64), (1, 4))),
        "grad_in": bell_draw(seeds[1], (TOKENS, FF), 1.0, 6.0, ((0, 64),)),
        "query_act": bell_draw(seeds[2], (QROWS, D), 1.0, 6.0, ((0, 64), (1, 4))),
        "query_grad": bell_draw(seeds[3], (QROWS, FF), 1.0, 6.0, ((0, 64),)),
        "act_basis": draw_act_basis(jax.random.fold_in(seeds[7], 71), 0),
        "grad_basis": draw_grad_basis(jax.random.fold_in(seeds[7], 71), 0),
        "seq_lengths": uneven(seeds[6], SEQS, SEQS * SEQ_LEN * 3 // 4, SEQ_LEN, 0).astype(jnp.int32),
    }


damping = 0.1

def rotate(rows_in, basis_rows):
    count_rows, full_width = rows_in.shape
    block_size = basis_rows.shape[1]
    blocks = full_width // block_size
    product = jnp.einsum('nbk,bkc->nbc', rows_in.reshape(count_rows, blocks, block_size).astype(jnp.float32), basis_rows.reshape(blocks, block_size, block_size).astype(jnp.float32))
    return product.reshape(count_rows, full_width)

def reference(act_in, grad_in, query_act, query_grad, act_basis, grad_basis, seq_lengths):
    position = jnp.arange(TOKENS, dtype=jnp.int32)
    seq_index = (position // SEQ_LEN).astype(jnp.int32)
    within = position % SEQ_LEN
    live_rows = (within < seq_lengths[seq_index]).astype(jnp.float32)
    act_rot = (rotate(act_in, act_basis) * live_rows[:, None]).astype(jnp.bfloat16)
    grad_rot = rotate(grad_in, grad_basis).astype(jnp.bfloat16)
    query_act_rot = rotate(query_act, act_basis).astype(jnp.bfloat16)
    query_grad_rot = rotate(query_grad, grad_basis).astype(jnp.bfloat16)
    act_square = jnp.square(act_rot.astype(jnp.float32)).astype(jnp.bfloat16)
    grad_square = jnp.square(grad_rot.astype(jnp.float32)).astype(jnp.bfloat16)
    counted = jnp.sum(seq_lengths).astype(jnp.float32)
    moments = jnp.dot(act_square.T, grad_square, preferred_element_type=jnp.float32) / counted
    weights = 1.0 / (moments + damping)
    scale_seq = lax.rsqrt(seq_lengths.astype(jnp.float32))

    def one_sequence(inputs):
        seq_acts, seq_grads, scale_one = inputs
        seq_grad = jnp.dot(seq_acts.T, seq_grads, preferred_element_type=jnp.float32)
        precond = (weights * seq_grad * scale_one).astype(jnp.bfloat16)
        mapped = jnp.dot(query_act_rot, precond, preferred_element_type=jnp.float32)
        per_row = lax.optimization_barrier(jnp.sum(mapped * query_grad_rot.astype(jnp.float32), axis=1))
        return lax.optimization_barrier(jnp.sum(per_row.reshape(QUERIES, QUERY_LEN), axis=1))
    columns = lax.map(one_sequence, (act_rot.reshape(SEQS, SEQ_LEN, D), grad_rot.reshape(SEQS, SEQ_LEN, FF), scale_seq))
    scores = columns.T / math.sqrt(QUERY_LEN * D * FF)
    return (moments, scores)
```

```python
import functools
import math

import jax
import jax.numpy as jnp
from jax import lax
from jax.experimental import pallas as pl
from jax.experimental.pallas import tpu as pltpu
from jax.sharding import Mesh
from jax.sharding import PartitionSpec as P

D = 4096
FF = 16384
BLOCK = 128
SEQS = 4
SEQ_LEN = 2048
TOKENS = 8192
QUERIES = 64
QUERY_LEN = 16
QROWS = 1024
RING = 4
TOK = 128
QTOK = 16
ROWS = TOK + QTOK
FEAT = 1024
HALF = 512
COLS = 256
UNIT = 512
KC = 256
Y, X, Z, H, C = "dp_0", "dp_1", "dp_2", "mp_0", "mp_1"
DP = (Y, X, Z)
MP = (H, C)
ALL = (Y, X, Z, H, C)
damping = 0.1


VM = pltpu.VMEM
SM = pltpu.SMEM
ANY = pl.ANY


def spec(space):
    return pl.BlockSpec(memory_space=space)


def dot(a, b, da, db):
    return lax.dot_general(
        a, b, (((da,), (db,)), ((), ())), preferred_element_type=jnp.float32
    )


def rotate_act_kernel(n_ref, act_ref, q_ref, basis_ref, out_ref):
    live = n_ref[0]
    mask = lax.broadcasted_iota(jnp.int32, (TOK, BLOCK), 0) < live
    for b in range(FEAT // BLOCK):
        cols = pl.ds(b * BLOCK, BLOCK)
        basis = basis_ref[cols, :]
        t = dot(act_ref[:, cols], basis, 1, 0)
        out_ref[0:TOK, cols] = jnp.where(mask, t, 0.0).astype(jnp.bfloat16)
        q = dot(q_ref[:, cols], basis, 1, 0)
        out_ref[TOK:ROWS, cols] = q.astype(jnp.bfloat16)


def rotate_act(n_live, act_in, query_act, act_basis):
    return pl.pallas_call(
        rotate_act_kernel,
        out_shape=jax.ShapeDtypeStruct((ROWS, FEAT), jnp.bfloat16),
        in_specs=[spec(SM), spec(VM), spec(VM), spec(VM)],
        out_specs=spec(VM),
        name="rotate_act",
    )(n_live, act_in, query_act, act_basis)


PACK = 8


def pack_kernel(c_ref, g_ref, q_ref, out_ref):
    for c in range(2):

        @pl.when(c_ref[0] == c)
        def _():
            for k in range(PACK):
                cols = pl.ds(k * COLS + c * BLOCK, BLOCK)
                out_ref[k, 0:TOK, :] = g_ref[:, cols]
                out_ref[k, TOK:ROWS, :] = q_ref[:, cols]


def pack(core, grad_in, query_grad):
    steps = FF // COLS // PACK
    return pl.pallas_call(
        pack_kernel,
        out_shape=jax.ShapeDtypeStruct((FF // COLS, ROWS, BLOCK), jnp.bfloat16),
        grid=(steps,),
        in_specs=[
            spec(SM),
            pl.BlockSpec((TOK, PACK * COLS), lambda i: (0, i)),
            pl.BlockSpec((QTOK, PACK * COLS), lambda i: (0, i)),
        ],
        out_specs=pl.BlockSpec((PACK, ROWS, BLOCK), lambda i: (i, 0, 0)),
        name="pack",
    )(core, grad_in, query_grad)


def rotate_grad_kernel(r_ref, basis_ref, out_ref, q_ref):
    basis_t = basis_ref[...].astype(jnp.float32).T.astype(jnp.bfloat16)
    group = 4

    @pl.loop(0, 64 // group)
    def _(i):
        rows = r_ref[pl.ds(i * group, group), 0:TOK, :].reshape(group * TOK, BLOCK)
        t = dot(basis_t, rows, 1, 1)
        at = pl.multiple_of(i * (group * TOK), group * TOK)
        out_ref[:, pl.ds(at, group * TOK)] = t.astype(jnp.bfloat16)
        for k in range(group):
            at = pl.multiple_of((i * group + k) * QTOK, QTOK)
            q_ref[pl.ds(at, QTOK), :] = r_ref[i * group + k, TOK:ROWS, :]

    q = dot(basis_t, q_ref[...], 1, 1)
    out_ref[:, pl.ds(TOKENS, QROWS)] = q.astype(jnp.bfloat16)


def rotate_grad(received, basis):
    return pl.pallas_call(
        rotate_grad_kernel,
        out_shape=jax.ShapeDtypeStruct((BLOCK, TOKENS + QROWS), jnp.bfloat16),
        in_specs=[spec(VM), spec(VM)],
        out_specs=spec(VM),
        scratch_shapes=[pltpu.VMEM((QROWS, BLOCK), jnp.bfloat16)],
        name="rotate_grad",
    )(received, basis)


def assemble_kernel(z_ref, *refs):
    ins, outs = refs[:RING], refs[RING:]
    for slot in range(RING):
        zb = lax.rem(z_ref[0] - slot + RING, RING)
        half, odd = zb // 2, lax.rem(zb, 2)
        at = pl.multiple_of(odd * TOK, TOK)
        qat = pl.multiple_of(2 * TOK + odd * QTOK, QTOK)
        for part in range(2):
            cols = pl.ds(part * HALF, HALF)
            outs[part][half, pl.ds(at, TOK), :] = ins[slot][0:TOK, cols]
            outs[part][half, pl.ds(qat, QTOK), :] = ins[slot][TOK:ROWS, cols]


UNIT_SHAPE = (2, 2 * ROWS, HALF)


def assemble(z, blocks):
    unit = jax.ShapeDtypeStruct(UNIT_SHAPE, jnp.bfloat16)
    return pl.pallas_call(
        assemble_kernel,
        out_shape=(unit, unit),
        in_specs=[spec(SM)] + [spec(VM)] * RING,
        out_specs=(spec(VM), spec(VM)),
        name="assemble",
    )(z, *blocks)


STEPS = (0, -1, 1, -2)


def copies_of(units, slots, coords_ref, act_ref, q_ref, sem, base):
    out = []
    for n, ((part, outer, inner), ref) in enumerate(units):
        first, second = (0, 1) if part == 0 else (1, 0)
        o = lax.rem(coords_ref[first] + STEPS[outer] + RING, RING)
        i = lax.rem(coords_ref[second] + STEPS[inner] + RING, RING)
        y, x = (o, i) if part == 0 else (i, o)
        block = y * RING + x
        for half in range(2):
            at = pl.multiple_of(block * UNIT + half * 256, 256)
            qat = pl.multiple_of(block * 64 + half * 32, 32)
            out.append(
                pltpu.make_async_copy(
                    ref.at[half, pl.ds(0, 256), :],
                    act_ref.at[part, pl.ds(at, 256), :],
                    sem.at[base + 4 * n + 2 * half],
                )
            )
            out.append(
                pltpu.make_async_copy(
                    ref.at[half, pl.ds(256, 32), :],
                    q_ref.at[part, pl.ds(qat, 32), :],
                    sem.at[base + 4 * n + 2 * half + 1],
                )
            )
    return out


def grad_copies(coords_ref, mine_ref, other_ref, g_ref, sem):
    c = coords_ref[2]
    a = pl.multiple_of(c * BLOCK, BLOCK)
    b = pl.multiple_of((1 - c) * BLOCK, BLOCK)
    return [
        pltpu.make_async_copy(mine_ref, g_ref.at[pl.ds(a, BLOCK), :], sem.at[0]),
        pltpu.make_async_copy(other_ref, g_ref.at[pl.ds(b, BLOCK), :], sem.at[1]),
    ]


def contract(part, seq, x, len_ref, act_ref, g_ref, mom_ref, seq_ref):
    left = jnp.clip(len_ref[seq] - x * UNIT, 0, UNIT)
    cols = pl.ds(part * HALF, HALF)

    @pl.loop(0, (left + KC - 1) // KC)
    def _(k):
        at = pl.multiple_of((seq * RING + x) * UNIT + k * KC, KC)
        a = act_ref[part, pl.ds(at, KC), :]
        g = g_ref[:, pl.ds(at, KC)]
        seq_ref[seq, :, cols] += dot(g, a, 1, 0)
        mom_ref[:, cols] += dot(g * g, a * a, 1, 0)


def first_kernel(keys, coords_ref, len_ref, mine_ref, other_ref, *refs):
    units = list(zip(keys, refs[: len(keys)]))
    mom_ref, seq_ref, q_ref, act_ref, g_ref, sem = refs[len(keys) :]
    copies = grad_copies(coords_ref, mine_ref, other_ref, g_ref, sem)
    copies += copies_of(units, None, coords_ref, act_ref, q_ref, sem, 2)
    for c in copies:
        c.start()
    mom_ref[...] = jnp.zeros_like(mom_ref)
    seq_ref[...] = jnp.zeros_like(seq_ref)
    for c in copies:
        c.wait()
    y, x = coords_ref[0], coords_ref[1]

    @pl.loop(0, 3)
    def _(o):
        far = o + o // 2

        @pl.loop(0, RING)
        def _(i):
            contract(0, lax.rem(y + far, RING), i, len_ref, act_ref, g_ref, mom_ref, seq_ref)
            contract(1, i, lax.rem(x + far, RING), len_ref, act_ref, g_ref, mom_ref, seq_ref)


def first(coords, lengths, mine, other, units):
    keys = tuple(units)
    return pl.pallas_call(
        functools.partial(first_kernel, keys),
        out_shape=(
            jax.ShapeDtypeStruct((COLS, FEAT), jnp.float32),
            jax.ShapeDtypeStruct((SEQS, COLS, FEAT), jnp.float32),
            jax.ShapeDtypeStruct((2, QROWS, HALF), jnp.bfloat16),
        ),
        in_specs=[spec(SM), spec(SM)] + [spec(ANY)] * (2 + len(keys)),
        out_specs=(spec(VM), spec(VM), spec(VM)),
        scratch_shapes=[
            pltpu.VMEM((2, TOKENS, HALF), jnp.bfloat16),
            pltpu.VMEM((COLS, TOKENS + QROWS), jnp.bfloat16),
            pltpu.SemaphoreType.DMA((2 + 4 * len(keys),)),
        ],
        compiler_params=pltpu.CompilerParams(vmem_limit_bytes=48 << 20),
        cost_estimate=pl.CostEstimate(
            flops=6 * TOKENS * FEAT * COLS // 2,
            bytes_accessed=24 << 20,
            transcendentals=0,
        ),
        name="first",
    )(coords, lengths, mine, other, *units.values())


def last_kernel(keys, coords_ref, len_ref, scale_ref, mine_ref, other_ref, mom_in, seq_in, q_in, *refs):
    units = list(zip(keys, refs[: len(keys)]))
    out_ref, score_ref, mom_ref, seq_ref, q_ref, act_ref, g_ref, sem = refs[len(keys) :]
    copies = grad_copies(coords_ref, mine_ref, other_ref, g_ref, sem)
    carried = [
        pltpu.make_async_copy(mom_in, mom_ref, sem.at[2]),
        pltpu.make_async_copy(seq_in, seq_ref, sem.at[3]),
        pltpu.make_async_copy(q_in, q_ref, sem.at[4]),
    ]
    copies += carried[:2]
    late = copies_of(units, None, coords_ref, act_ref, q_ref, sem, 5)
    carried[2].start()
    for c in copies:
        c.start()
    carried[2].wait()
    for c in late:
        c.start()
    for c in copies + late:
        c.wait()
    y, x = coords_ref[0], coords_ref[1]

    @pl.loop(0, RING)
    def _(i):
        contract(0, lax.rem(y + 2, RING), i, len_ref, act_ref, g_ref, mom_ref, seq_ref)
        contract(1, i, lax.rem(x + 2, RING), len_ref, act_ref, g_ref, mom_ref, seq_ref)

    for k in range(FEAT // COLS):
        cols = pl.ds(k * COLS, COLS)
        m = mom_ref[:, cols] / scale_ref[SEQS]
        out_ref[cols, :] = m.T
        mom_ref[:, cols] = 1.0 / (m + damping)

    @pl.loop(0, SEQS)
    def _(s):
        total = jnp.zeros((COLS, QROWS), jnp.float32)
        for part in range(2):
            cols = pl.ds(part * HALF, HALF)
            p = mom_ref[:, cols] * seq_ref[s, :, cols] * scale_ref[s]
            total += dot(p.astype(jnp.bfloat16), q_ref[part], 1, 1)
        qg = g_ref[:, pl.ds(TOKENS, QROWS)].astype(jnp.float32)
        score_ref[pl.ds(s, 1), :] = jnp.sum(total * qg, axis=0, keepdims=True)


def last(coords, lengths, scales, mine, other, carried, units):
    keys = tuple(units)
    return pl.pallas_call(
        functools.partial(last_kernel, keys),
        out_shape=(
            jax.ShapeDtypeStruct((FEAT, COLS), jnp.float32),
            jax.ShapeDtypeStruct((SEQS, QROWS), jnp.float32),
        ),
        in_specs=[spec(SM), spec(SM), spec(SM)] + [spec(ANY)] * (5 + len(keys)),
        out_specs=(spec(VM), spec(VM)),
        scratch_shapes=[
            pltpu.VMEM((COLS, FEAT), jnp.float32),
            pltpu.VMEM((SEQS, COLS, FEAT), jnp.float32),
            pltpu.VMEM((2, QROWS, HALF), jnp.bfloat16),
            pltpu.VMEM((2, TOKENS, HALF), jnp.bfloat16),
            pltpu.VMEM((COLS, TOKENS + QROWS), jnp.bfloat16),
            pltpu.SemaphoreType.DMA((5 + 4 * len(keys),)),
        ],
        compiler_params=pltpu.CompilerParams(vmem_limit_bytes=52 << 20),
        name="last",
    )(coords, lengths, scales, mine, other, *carried, *units.values())


def shift(x, axis, step):
    return lax.ppermute(x, axis, [(i, (i + step) % RING) for i in range(RING)])


def around(own, axis):
    left, right = shift(own, axis, 1), shift(own, axis, -1)
    far = jnp.stack([shift(left[0], axis, 1), shift(right[1], axis, -1)])
    return [own, left, right, far]


def spread(part, own, inner_axis, outer_axis):
    inner = around(own, inner_axis)
    left = [shift(u, outer_axis, 1) for u in inner]
    right = [shift(u, outer_axis, -1) for u in inner]
    far = [
        shift(left[0], outer_axis, 1),
        shift(left[1], outer_axis, 1),
        shift(right[2], outer_axis, -1),
        shift(right[3], outer_axis, -1),
    ]
    groups = [inner, left, right, far]
    return {
        (part, o, i): groups[o][i] for o in range(RING) for i in range(RING)
    }


def local(act_in, grad_in, query_act, query_grad, act_basis, grad_basis, seq_lengths):
    y, x, z, core = (lax.axis_index(a) for a in (Y, X, Z, C))
    chunk = x * RING + z
    n_live = jnp.clip(seq_lengths[y] - chunk * TOK, 0, TOK).reshape(1)
    own = rotate_act(n_live, act_in, query_act, act_basis)
    blocks = [own] + [shift(own, Z, s) for s in range(1, RING)]

    packed = pack(core.reshape(1), grad_in, query_grad)
    received = lax.all_to_all(packed, DP, 0, 0, tiled=True)
    basis = lax.dynamic_slice(grad_basis, (core * BLOCK, 0), (BLOCK, BLOCK))
    mine = rotate_grad(received, basis)
    other = lax.ppermute(mine, C, [(0, 1), (1, 0)])

    part_a, part_b = assemble(z.reshape(1), blocks)
    units = spread(0, part_a, X, Y)
    units.update(spread(1, part_b, Y, X))
    early = {k: v for k, v in units.items() if k[1] < 3}
    late = {k: v for k, v in units.items() if k[1] == 3}

    coords = jnp.stack([y, x, core])
    counted = jnp.sum(seq_lengths).astype(jnp.float32)
    scales = jnp.concatenate(
        [lax.rsqrt(seq_lengths.astype(jnp.float32)), counted[None]]
    )
    carried = first(coords, seq_lengths, mine, other, early)
    moments, per_row = last(coords, seq_lengths, scales, mine, other, carried, late)
    per_query = jnp.sum(per_row.reshape(SEQS, QUERIES, QUERY_LEN), axis=2)
    partial = per_query.reshape(2, 128) / math.sqrt(QUERY_LEN * D * FF)
    everywhere = jnp.broadcast_to(partial[None], (256, 2, 128))
    scores = lax.all_to_all(everywhere, ALL, 0, 0, tiled=True).sum(0)
    return moments, scores.reshape(SEQS, QUERIES).T


def solution(mesh):
    finer = Mesh(mesh.devices.reshape(4, 4, 4, 2, 2), ALL)
    placed = (P(DP, MP), P(DP, None), P(DP, MP), P(DP, None), P(MP, None), P(DP, None), P())
    return jax.shard_map(
        local, mesh=finer, in_specs=placed, out_specs=(P(MP, DP), P()), check_vma=False
    )
```

```python
import functools
import math

import jax
import jax.numpy as jnp
from jax import lax
from jax.experimental import pallas as pl
from jax.experimental.pallas import tpu as pltpu
from jax.sharding import Mesh
from jax.sharding import PartitionSpec as P

D = 4096
FF = 16384
BLOCK = 128
SEQS = 4
TOKENS = 8192
QUERIES = 64
QUERY_LEN = 16
QROWS = 1024
RING = 4
TOK = 128
QTOK = 16
ROWS = TOK + QTOK
FEAT = 1024
HALF = 512
COLS = 256
UNIT = 512
KC = 256
PLANE = 16
Y, X, Z, H, C = "dp_0", "dp_1", "dp_2", "mp_0", "mp_1"
DP = (Y, X, Z)
MP = (H, C)
ALL = (Y, X, Z, H, C)
damping = 0.1


VM = pltpu.VMEM
SM = pltpu.SMEM
ANY = pl.ANY


def spec(space):
    return pl.BlockSpec(memory_space=space)


def dot(a, b, da, db):
    return lax.dot_general(
        a, b, (((da,), (db,)), ((), ())), preferred_element_type=jnp.float32
    )


def rotate_act_kernel(n_ref, act_ref, q_ref, basis_ref, out_ref):
    live = n_ref[0]
    mask = lax.broadcasted_iota(jnp.int32, (TOK, BLOCK), 0) < live
    for b in range(FEAT // BLOCK):
        cols = pl.ds(b * BLOCK, BLOCK)
        basis = basis_ref[cols, :]
        t = dot(act_ref[:, cols], basis, 1, 0)
        out_ref[0:TOK, cols] = jnp.where(mask, t, 0.0).astype(jnp.bfloat16)
        q = dot(q_ref[:, cols], basis, 1, 0)
        out_ref[TOK:ROWS, cols] = q.astype(jnp.bfloat16)


def rotate_act(n_live, act_in, query_act, act_basis):
    return pl.pallas_call(
        rotate_act_kernel,
        out_shape=jax.ShapeDtypeStruct((ROWS, FEAT), jnp.bfloat16),
        in_specs=[spec(SM), spec(VM), spec(VM), spec(VM)],
        out_specs=spec(VM),
        name="rotate_act",
    )(n_live, act_in, query_act, act_basis)


def pack_kernel(coords_ref, g_ref, q_ref, after_ref, out_ref):
    for c in range(2):

        @pl.when(coords_ref[3] == c)
        def _():
            for k in range(2 * RING):
                step = lax.rem(k % RING - coords_ref[2] + RING, RING)
                cols = pl.ds(k * COLS + c * BLOCK, BLOCK)
                out_ref[k // RING, step, 0:TOK, :] = g_ref[:, cols]
                out_ref[k // RING, step, TOK:ROWS, :] = q_ref[:, cols]


def pack(coords, grad_in, query_grad, after):
    return pl.pallas_call(
        pack_kernel,
        out_shape=jax.ShapeDtypeStruct((PLANE, RING, ROWS, BLOCK), jnp.bfloat16),
        grid=(PLANE // 2,),
        in_specs=[
            spec(SM),
            pl.BlockSpec((TOK, 2 * RING * COLS), lambda i: (0, i)),
            pl.BlockSpec((QTOK, 2 * RING * COLS), lambda i: (0, i)),
            spec(ANY),
        ],
        out_specs=pl.BlockSpec((2, RING, ROWS, BLOCK), lambda i: (i, 0, 0, 0)),
        name="pack",
    )(coords, grad_in, query_grad, after)


def rotate_grad_kernel(coords_ref, own_ref, prev_ref, next_ref, far0_ref, far1_ref, basis_ref, out_ref, q_ref):
    basis_t = basis_ref[...].astype(jnp.float32).T.astype(jnp.bfloat16)
    group = 4
    z = coords_ref[2]
    sources = ((own_ref, 0, 0), (prev_ref, 3, 0), (next_ref, 1, 0), (far0_ref, 2, 0), (far1_ref, 2, 8))
    for ref, step, base in sources:
        src = lax.rem(z + step, RING)

        @pl.loop(0, ref.shape[0] // group)
        def _(i):
            rows = ref[pl.ds(i * group, group), 0:TOK, :].reshape(group * TOK, BLOCK)
            t = dot(basis_t, rows, 1, 1).astype(jnp.bfloat16)
            for k in range(group):
                block = (base + i * group + k) * RING + src
                at = pl.multiple_of(block * TOK, TOK)
                out_ref[:, pl.ds(at, TOK)] = t[:, k * TOK : (k + 1) * TOK]
                at = pl.multiple_of(block * QTOK, QTOK)
                q_ref[pl.ds(at, QTOK), :] = ref[i * group + k, TOK:ROWS, :]

    q = dot(basis_t, q_ref[...], 1, 1)
    out_ref[:, pl.ds(TOKENS, QROWS)] = q.astype(jnp.bfloat16)


def rotate_grad(coords, parts, basis):
    return pl.pallas_call(
        rotate_grad_kernel,
        out_shape=jax.ShapeDtypeStruct((BLOCK, TOKENS + QROWS), jnp.bfloat16),
        in_specs=[spec(SM)] + [spec(VM)] * 6,
        out_specs=spec(VM),
        scratch_shapes=[pltpu.VMEM((QROWS, BLOCK), jnp.bfloat16)],
        cost_estimate=pl.CostEstimate(
            flops=2 * (TOKENS + QROWS) * BLOCK * BLOCK,
            bytes_accessed=5 << 20,
            transcendentals=0,
        ),
        name="rotate_grad",
    )(coords, *parts, basis)


def assemble_kernel(z_ref, *refs):
    ins, outs = refs[:RING], refs[RING:]
    for slot in range(RING):
        zb = lax.rem(z_ref[0] - slot + RING, RING)
        half, odd = zb // 2, lax.rem(zb, 2)
        at = pl.multiple_of(odd * TOK, TOK)
        qat = pl.multiple_of(2 * TOK + odd * QTOK, QTOK)
        for part in range(2):
            cols = pl.ds(part * HALF, HALF)
            outs[part][half, pl.ds(at, TOK), :] = ins[slot][0:TOK, cols]
            outs[part][half, pl.ds(qat, QTOK), :] = ins[slot][TOK:ROWS, cols]


UNIT_SHAPE = (2, 2 * ROWS, HALF)


def assemble(z, blocks):
    unit = jax.ShapeDtypeStruct(UNIT_SHAPE, jnp.bfloat16)
    return pl.pallas_call(
        assemble_kernel,
        out_shape=(unit, unit),
        in_specs=[spec(SM)] + [spec(VM)] * RING,
        out_specs=(spec(VM), spec(VM)),
        name="assemble",
    )(z, *blocks)


STEPS = (0, -1, 1, -2)


def place(at, slot):
    return lax.rem(at + STEPS[slot] + RING, RING)


def contract(unit, seq, x, len_ref, mine_ref, other_ref, mom_ref, seq_ref, seq_at):
    left = jnp.clip(len_ref[seq] - x * UNIT, 0, UNIT)

    @pl.loop(0, (left + KC - 1) // KC)
    def _(h):
        at = pl.multiple_of((seq * RING + x) * UNIT + h * KC, KC)
        a = unit[h, 0:KC, :]
        g = jnp.concatenate([mine_ref[:, pl.ds(at, KC)], other_ref[:, pl.ds(at, KC)]])
        seq_ref[seq_at] += dot(g, a, 1, 0)
        mom_ref[...] += dot(g * g, a * a, 1, 0)


def take(unit, at, q_ref):
    for h in range(2):
        row = pl.multiple_of(at + h * 32, 32)
        q_ref[pl.ds(row, 32), :] = unit[h, KC : KC + 32, :]


def group_kernel(part, outer, coords_ref, len_ref, mine_ref, other_ref, *refs):
    units, refs = refs[:RING], refs[RING:]
    if outer:
        refs = refs[1:] if part == 0 else refs[2:]
    mom_ref, seq_ref, q_ref = refs
    if not outer:
        mom_ref[...] = jnp.zeros_like(mom_ref)
    if not (outer and part):
        seq_ref[...] = jnp.zeros_like(seq_ref)
    y, x = coords_ref[0], coords_ref[1]
    for i, unit in enumerate(units):
        if part == 0:
            seq, xb = place(y, outer), place(x, i)
            take(unit, xb * 64, q_ref)
            contract(unit, seq, xb, len_ref, mine_ref, other_ref, mom_ref, seq_ref, 0)
        else:
            seq, xb = place(y, i), place(x, outer)
            take(unit, seq * 64, q_ref)
            contract(unit, seq, xb, len_ref, mine_ref, other_ref, mom_ref, seq_ref, seq)


def group(part, outer, coords, lengths, mine, other, units, mom, seqs):
    seq_rows = 1 if part == 0 else SEQS
    carried = [] if outer == 0 else [mom] if part == 0 else [mom, seqs]
    base = 4 + RING
    return pl.pallas_call(
        functools.partial(group_kernel, part, outer),
        out_shape=(
            jax.ShapeDtypeStruct((COLS, HALF), jnp.float32),
            jax.ShapeDtypeStruct((seq_rows, COLS, HALF), jnp.float32),
            jax.ShapeDtypeStruct((256, HALF), jnp.bfloat16),
        ),
        in_specs=[spec(SM)] * 2 + [spec(VM)] * (2 + RING + len(carried)),
        out_specs=(spec(VM),) * 3,
        input_output_aliases={base + k: k for k in range(len(carried))},
        compiler_params=pltpu.CompilerParams(vmem_limit_bytes=24 << 20),
        cost_estimate=pl.CostEstimate(
            flops=4 * TOKENS * HALF * COLS // 4,
            bytes_accessed=10 << 20,
            transcendentals=0,
        ),
    )(coords, lengths, mine, other, *units, *carried)


def last_kernel(coords_ref, len_ref, scale_ref, mine_ref, other_ref, *refs):
    units_a, units_b, refs = refs[:RING], refs[RING : 2 * RING], refs[2 * RING :]
    mom_a, mom_b, seq_a, seq_b, q_a, q_b, refs = (
        refs[0], refs[1], refs[2:5], refs[5], refs[6:9], refs[9:12], refs[12:],
    )
    out_ref, score_ref, w_ref, far_ref, sb_ref, q_ref = refs
    y, x, c = coords_ref[0], coords_ref[1], coords_ref[3]
    w_ref[0] = mom_a[...]
    w_ref[1] = mom_b[...]
    sb_ref[...] = seq_b[...]
    far_ref[...] = jnp.zeros_like(far_ref)
    for o in range(3):
        at = pl.multiple_of(place(y, o) * 256, 256)
        q_ref[0, pl.ds(at, 256), :] = q_a[o][...]
        for s in range(SEQS):
            at = pl.multiple_of(s * 256 + place(x, o) * 64, 64)
            q_ref[1, pl.ds(at, 64), :] = q_b[o][s * 64 : (s + 1) * 64, :]
    for i in range(RING):
        seq, xb = place(y, 3), place(x, i)
        take(units_a[i], seq * 256 + xb * 64, q_ref.at[0])
        contract(units_a[i], seq, xb, len_ref, mine_ref, other_ref, w_ref.at[0], far_ref, 0)
        seq, xb = place(y, i), place(x, 3)
        take(units_b[i], seq * 256 + xb * 64, q_ref.at[1])
        contract(units_b[i], seq, xb, len_ref, mine_ref, other_ref, w_ref.at[1], sb_ref, seq)

    mine_at = pl.multiple_of(c * BLOCK, BLOCK)
    other_at = pl.multiple_of((1 - c) * BLOCK, BLOCK)
    for part in range(2):
        for k in range(HALF // 256):
            cols = pl.ds(k * 256, 256)
            m = w_ref[part, :, cols] / scale_ref[SEQS]
            rows = pl.ds(part * HALF + k * 256, 256)
            out_ref[rows, pl.ds(mine_at, BLOCK)] = m[0:BLOCK, :].T
            out_ref[rows, pl.ds(other_at, BLOCK)] = m[BLOCK:COLS, :].T
            w_ref[part, :, cols] = 1.0 / (m + damping)

    score_ref[...] = jnp.zeros_like(score_ref)

    def score(part, grads, s):
        p = (w_ref[part] * grads * scale_ref[s]).astype(jnp.bfloat16)
        for k in range(2):
            rows = pl.ds(k * 512, 512)
            mapped = dot(p, q_ref[part, rows, :], 1, 1)
            at = pl.ds(TOKENS + k * 512, 512)
            total = jnp.sum(mapped[0:BLOCK] * mine_ref[:, at].astype(jnp.float32), axis=0, keepdims=True)
            total += jnp.sum(mapped[BLOCK:COLS] * other_ref[:, at].astype(jnp.float32), axis=0, keepdims=True)
            score_ref[pl.ds(s, 1), rows] += total

    for o in range(3):
        score(0, seq_a[o][0], place(y, o))
    score(0, far_ref[0], place(y, 3))

    @pl.loop(0, SEQS)
    def _(s):
        score(1, sb_ref[s], s)


def last(coords, lengths, scales, mine, other, units, carried):
    return pl.pallas_call(
        last_kernel,
        out_shape=(
            jax.ShapeDtypeStruct((FEAT, COLS), jnp.float32),
            jax.ShapeDtypeStruct((SEQS, QROWS), jnp.float32),
        ),
        in_specs=[spec(SM)] * 3 + [spec(VM)] * (2 + len(units) + len(carried)),
        out_specs=(spec(VM), spec(VM)),
        scratch_shapes=[
            pltpu.VMEM((2, COLS, HALF), jnp.float32),
            pltpu.VMEM((1, COLS, HALF), jnp.float32),
            pltpu.VMEM((SEQS, COLS, HALF), jnp.float32),
            pltpu.VMEM((2, QROWS, HALF), jnp.bfloat16),
        ],
        compiler_params=pltpu.CompilerParams(vmem_limit_bytes=32 << 20),
        name="last",
    )(coords, lengths, scales, mine, other, *units, *carried)


def shift(x, axis, step):
    return lax.ppermute(x, axis, [(i, (i + step) % RING) for i in range(RING)])


def around(own, axis):
    left, right = shift(own, axis, 1), shift(own, axis, -1)
    far_left = shift(left[0], axis, 1)
    far_right = shift(right[1], axis, -1)
    return [own, left, right, jnp.stack([far_left, far_right])]


def spread(own, inner_axis, outer_axis):
    inner = around(own, inner_axis)
    left = [shift(u, outer_axis, 1) for u in inner]
    right = [shift(u, outer_axis, -1) for u in inner]
    far = [
        shift(left[0], outer_axis, 1),
        shift(left[1], outer_axis, 1),
        shift(right[2], outer_axis, -1),
        shift(right[3], outer_axis, -1),
    ]
    return [inner, left, right, far]


def at_z(k):
    k %= 2 * RING
    return k % RING * 2 + k // RING


def along_z(x, step):
    return lax.ppermute(x, (Z, H), [(at_z(k), at_z(k + step)) for k in range(2 * RING)])


def local(act_in, grad_in, query_act, query_grad, act_basis, grad_basis, seq_lengths):
    y, x, z, core = (lax.axis_index(a) for a in (Y, X, Z, C))
    coords = jnp.stack([y, x, z, core])
    chunk = x * RING + z
    n_live = jnp.clip(seq_lengths[y] - chunk * TOK, 0, TOK).reshape(1)
    own = rotate_act(n_live, act_in, query_act, act_basis)
    blocks = [own] + [shift(own, Z, s) for s in range(1, RING)]

    packed = pack(coords, grad_in, query_grad, own)
    packed = packed.reshape(PLANE, RING * ROWS, BLOCK)
    received = lax.all_to_all(packed, (Y, X), 0, 0, tiled=True)
    received = received.reshape(PLANE, RING, ROWS, BLOCK)
    parts = [
        received[:, 0],
        along_z(received[:, 1], 1),
        along_z(received[:, 3], -1),
        along_z(received[:8, 2], 2),
        along_z(received[8:, 2], -2),
    ]
    basis = lax.dynamic_slice(grad_basis, (core * BLOCK, 0), (BLOCK, BLOCK))
    mine = rotate_grad(coords, parts, basis)
    other = lax.ppermute(mine, C, [(0, 1), (1, 0)])

    part_a, part_b = assemble(z.reshape(1), blocks)
    units = (spread(part_a, X, Y), spread(part_b, Y, X))
    moms, seqs, queries = [None, None], [[], []], [[], []]
    for outer in range(3):
        for part in range(2):
            last_seqs = seqs[part][-1] if outer else None
            moms[part], s, q = group(part, outer, coords, seq_lengths, mine, other, units[part][outer], moms[part], last_seqs)
            seqs[part].append(s)
            queries[part].append(q)

    counted = jnp.sum(seq_lengths).astype(jnp.float32)
    scales = jnp.concatenate(
        [lax.rsqrt(seq_lengths.astype(jnp.float32)), counted[None]]
    )
    carried = [*moms, *seqs[0], seqs[1][-1], *queries[0], *queries[1]]
    far = [*units[0][3], *units[1][3]]
    moments, per_row = last(coords, seq_lengths, scales, mine, other, far, carried)
    per_query = jnp.sum(per_row.reshape(SEQS, QUERIES, QUERY_LEN), axis=2)
    partial = per_query.reshape(2, 128) / math.sqrt(QUERY_LEN * D * FF)
    everywhere = jnp.broadcast_to(partial[None], (256, 2, 128))
    scores = lax.all_to_all(everywhere, ALL, 0, 0, tiled=True).sum(0)
    return moments, scores.reshape(SEQS, QUERIES).T


def solution(mesh):
    finer = Mesh(mesh.devices.reshape(4, 4, 4, 2, 2), ALL)
    placed = (P(DP, MP), P(DP, None), P(DP, MP), P(DP, None), P(MP, None), P(DP, None), P())

    return jax.shard_map(
        local, mesh=finer, in_specs=placed, out_specs=(P(MP, DP), P()), check_vma=False
    )
```

```python
import functools
import math

import jax
import jax.numpy as jnp
from jax import lax
from jax.experimental import pallas as pl
from jax.experimental.pallas import tpu as pltpu
from jax.sharding import Mesh
from jax.sharding import PartitionSpec as P

D = 4096
FF = 16384
BLOCK = 128
SEQS = 4
SEQ_LEN = 2048
TOKENS = 8192
QUERIES = 64
QUERY_LEN = 16
QROWS = 1024
RING = 4
TOK = 128
QTOK = 16
ROWS = TOK + QTOK
FEAT = 1024
HALF = 512
COLS = 256
UNIT = 512
KC = 256
PLANE = 16
Y, X, Z, H, C = "dp_0", "dp_1", "dp_2", "mp_0", "mp_1"
DP = (Y, X, Z)
MP = (H, C)
ALL = (Y, X, Z, H, C)
damping = 0.1


VM = pltpu.VMEM
SM = pltpu.SMEM
ANY = pl.ANY


def spec(space):
    return pl.BlockSpec(memory_space=space)


def dot(a, b, da, db):
    return lax.dot_general(
        a, b, (((da,), (db,)), ((), ())), preferred_element_type=jnp.float32
    )


def where():
    return tuple(lax.axis_index(a) for a in (Y, X, Z, H, C))


def rotate_act_kernel(len_ref, act_ref, q_ref, basis_ref, out_ref):
    y, x, z, _, _ = where()
    live = jnp.clip(len_ref[y] - (x * RING + z) * TOK, 0, TOK)
    mask = lax.broadcasted_iota(jnp.int32, (TOK, BLOCK), 0) < live
    for b in range(FEAT // BLOCK):
        cols = pl.ds(b * BLOCK, BLOCK)
        basis = basis_ref[cols, :]
        t = dot(act_ref[:, cols], basis, 1, 0)
        out_ref[0:TOK, cols] = jnp.where(mask, t, 0.0).astype(jnp.bfloat16)
        q = dot(q_ref[:, cols], basis, 1, 0)
        out_ref[TOK:ROWS, cols] = q.astype(jnp.bfloat16)


def rotate_act(lengths, act_in, query_act, act_basis):
    return pl.pallas_call(
        rotate_act_kernel,
        out_shape=jax.ShapeDtypeStruct((ROWS, FEAT), jnp.bfloat16),
        in_specs=[spec(SM), spec(VM), spec(VM), spec(VM)],
        out_specs=spec(VM),
        name="rotate_act",
    )(lengths, act_in, query_act, act_basis)


PART = ROWS // 2
SENT = 2 * ROWS + PART


def pack_kernel(g_ref, q_ref, after_ref, out_ref, sem):
    _, _, z, h, c = where()
    copies = []

    def send(src, dst):
        copies.append(pltpu.make_async_copy(src, dst, sem.at[len(copies)]))

    for n in range(PLANE):

        def cols(step):
            at = n * RING * COLS + lax.rem(z + step, RING) * COLS + c * BLOCK
            return pl.ds(pl.multiple_of(at, BLOCK), BLOCK)

        odd = cols(1 + 2 * h)
        send(g_ref.at[:, cols(0)], out_ref.at[n, pl.ds(0, TOK), :])
        send(q_ref.at[:, cols(0)], out_ref.at[n, pl.ds(TOK, QTOK), :])
        send(g_ref.at[:, odd], out_ref.at[n, pl.ds(ROWS, TOK), :])
        send(q_ref.at[:, odd], out_ref.at[n, pl.ds(ROWS + TOK, QTOK), :])
    for copy in copies:
        copy.start()

    def half(n, pieces):
        at = n * RING * COLS + lax.rem(z + 2, RING) * COLS + c * BLOCK
        cols = pl.ds(pl.multiple_of(at, BLOCK), BLOCK)
        return [
            pltpu.make_async_copy(
                ref.at[rows, cols], out_ref.at[n, to, :], sem.at[4 * PLANE + 2 * n + k]
            )
            for k, (ref, rows, to) in enumerate(pieces)
        ]

    cut = 2 * ROWS + TOK - PART
    halves = (
        ((g_ref, pl.ds(0, PART), pl.ds(2 * ROWS, PART)),),
        (
            (g_ref, pl.ds(PART, TOK - PART), pl.ds(2 * ROWS, TOK - PART)),
            (q_ref, pl.ds(0, QTOK), pl.ds(cut, QTOK)),
        ),
    )
    for k in range(2):

        @pl.when(h == k)
        def _():
            rest = [copy for n in range(PLANE) for copy in half(n, halves[k])]
            for copy in rest:
                copy.start()
            for copy in rest:
                copy.wait()

    for copy in copies:
        copy.wait()


def pack(grad_in, query_grad, after):
    return pl.pallas_call(
        pack_kernel,
        out_shape=jax.ShapeDtypeStruct((PLANE, SENT, BLOCK), jnp.bfloat16),
        in_specs=[spec(ANY)] * 3,
        out_specs=spec(VM),
        scratch_shapes=[pltpu.SemaphoreType.DMA((6 * PLANE,))],
        name="pack",
    )(grad_in, query_grad, after)


def rotate_grad_kernel(own_ref, u1_ref, u2_ref, f1_ref, f2_ref, basis_ref, out_ref, q_ref, far_ref):
    _, _, z, h, c = where()
    at = pl.multiple_of(c * BLOCK, BLOCK)
    basis_t = basis_ref[pl.ds(at, BLOCK), :].astype(jnp.float32).T.astype(jnp.bfloat16)
    p = h * RING + z
    first = jnp.logical_and(p >= 2, p < 6)

    @pl.when(first)
    def _():
        far_ref[:, 0:PART, :] = f1_ref[...]
        far_ref[:, PART:ROWS, :] = f2_ref[...]

    @pl.when(jnp.logical_not(first))
    def _():
        far_ref[:, 0:PART, :] = f2_ref[...]
        far_ref[:, PART:ROWS, :] = f1_ref[...]

    below = jnp.logical_and(p >= 1, p < 5)
    step = jnp.where(below, 3, 1)
    group = 4
    for ref, s in ((own_ref, 0), (u1_ref, step), (u2_ref, RING - step), (far_ref, 2)):
        src = lax.rem(z + s, RING)

        @pl.loop(0, PLANE // group)
        def _(i):
            rows = ref[pl.ds(i * group, group), 0:TOK, :].reshape(group * TOK, BLOCK)
            t = dot(basis_t, rows, 1, 1).astype(jnp.bfloat16)
            for k in range(group):
                block = (i * group + k) * RING + src
                at = pl.multiple_of(block * TOK, TOK)
                out_ref[:, pl.ds(at, TOK)] = t[:, k * TOK : (k + 1) * TOK]
                at = pl.multiple_of(block * QTOK, QTOK)
                q_ref[pl.ds(at, QTOK), :] = ref[i * group + k, TOK:ROWS, :]

    q = dot(basis_t, q_ref[...], 1, 1)
    out_ref[:, pl.ds(TOKENS, QROWS)] = q.astype(jnp.bfloat16)


def rotate_grad(parts, basis):
    return pl.pallas_call(
        rotate_grad_kernel,
        out_shape=jax.ShapeDtypeStruct((BLOCK, TOKENS + QROWS), jnp.bfloat16),
        in_specs=[spec(VM)] * 6,
        out_specs=spec(VM),
        scratch_shapes=[
            pltpu.VMEM((QROWS, BLOCK), jnp.bfloat16),
            pltpu.VMEM((PLANE, ROWS, BLOCK), jnp.bfloat16),
        ],
        compiler_params=pltpu.CompilerParams(vmem_limit_bytes=16 << 20),
        cost_estimate=pl.CostEstimate(
            flops=2 * (TOKENS + QROWS) * BLOCK * BLOCK,
            bytes_accessed=5 << 20,
            transcendentals=0,
        ),
        name="rotate_grad",
    )(*parts, basis)


def assemble_kernel(*refs):
    ins, outs = refs[:RING], refs[RING:]
    z = lax.axis_index(Z)
    for slot in range(RING):
        zb = lax.rem(z - slot + RING, RING)
        half, odd = zb // 2, lax.rem(zb, 2)
        at = pl.multiple_of(odd * TOK, TOK)
        qat = pl.multiple_of(2 * TOK + odd * QTOK, QTOK)
        for part in range(2):
            cols = pl.ds(part * HALF, HALF)
            outs[part][half, pl.ds(at, TOK), :] = ins[slot][0:TOK, cols]
            outs[part][half, pl.ds(qat, QTOK), :] = ins[slot][TOK:ROWS, cols]


def assemble(blocks):
    unit = jax.ShapeDtypeStruct((2, 2 * ROWS, HALF), jnp.bfloat16)
    return pl.pallas_call(
        assemble_kernel,
        out_shape=(unit, unit),
        in_specs=[spec(VM)] * RING,
        out_specs=(spec(VM), spec(VM)),
        compiler_params=pltpu.CompilerParams(vmem_limit_bytes=8 << 20),
        name="assemble",
    )(*blocks)


def join_kernel(a_ref, b_ref, out_ref, sem):
    copies = [
        pltpu.make_async_copy(ref, out_ref.at[pl.ds(2 * n, 2)], sem.at[n])
        for n, ref in enumerate((a_ref, b_ref))
    ]
    for c in copies:
        c.start()
    for c in copies:
        c.wait()


def join(a, b):
    return pl.pallas_call(
        join_kernel,
        out_shape=jax.ShapeDtypeStruct((4, 2 * ROWS, HALF), jnp.bfloat16),
        in_specs=[spec(ANY)] * 2,
        out_specs=spec(VM),
        scratch_shapes=[pltpu.SemaphoreType.DMA((2,))],
        compiler_params=pltpu.CompilerParams(vmem_limit_bytes=4 << 20),
        name="join",
    )(a, b)


def place(at, slot):
    return lax.rem(at - slot + RING, RING)


HALVES = 2 * RING


def group_copies(part, outer, pair_refs, grad_refs, u_ref, g_ref, sem):
    y, x, _, _, _ = where()
    out = [
        pltpu.make_async_copy(ref, u_ref.at[pl.ds(4 * n, 4)], sem.at[n])
        for n, ref in enumerate(pair_refs)
    ]
    for m, ref in enumerate(grad_refs):
        if part == 0:
            at = pl.multiple_of(place(y, outer) * SEQ_LEN, SEQ_LEN)
            out.append(pltpu.make_async_copy(ref.at[:, pl.ds(at, SEQ_LEN)], g_ref.at[m], sem.at[2 + RING * m]))
            continue
        for s in range(SEQS):
            at = pl.multiple_of(s * SEQ_LEN + place(x, outer) * UNIT, UNIT)
            out.append(pltpu.make_async_copy(ref.at[:, pl.ds(at, UNIT)], g_ref.at[m, :, pl.ds(s * UNIT, UNIT)], sem.at[2 + RING * m + s]))
    return out


SEMS = 2 + 2 * RING


def contract(part, outer, len_ref, u_ref, g_ref, mom_ref, seq_ref, q_ref):
    y, x, _, _, _ = where()

    @pl.loop(0, HALVES)
    def _(n):
        v = place(x if part == 0 else y, n // 2)
        half = lax.rem(n, 2)
        seq, block = (place(y, outer), v) if part == 0 else (v, place(x, outer))
        q_at = v * 64 if part == 0 else v * 256 + block * 64
        q_at = pl.multiple_of(q_at + half * 32, 32)
        q_ref[pl.ds(q_at, 32), :] = u_ref[n, KC : KC + 32, :]

        @pl.when(len_ref[seq] > block * UNIT + half * KC)
        def _():
            at = pl.multiple_of(v * UNIT + half * KC, KC)
            a = u_ref[n, 0:KC, :]
            g = jnp.concatenate([g_ref[0, :, pl.ds(at, KC)], g_ref[1, :, pl.ds(at, KC)]])
            seq_ref[seq if part else 0] += dot(g, a, 1, 0)
            mom_ref[...] += dot(g * g, a * a, 1, 0)


def group_kernel(part, outer, len_ref, mine_ref, other_ref, p_ref, q_ref, *refs):
    carried = 0 if outer == 0 else 2 if part == 0 else 3
    refs = refs[carried:]
    mom_ref, seq_ref, qout_ref, u_ref, g_ref, sem = refs
    copies = group_copies(part, outer, (p_ref, q_ref), (mine_ref, other_ref), u_ref, g_ref, sem)
    for c in copies:
        c.start()
    if not outer:
        mom_ref[...] = jnp.zeros_like(mom_ref)
    if not (outer and part):
        seq_ref[...] = jnp.zeros_like(seq_ref)
    for c in copies:
        c.wait()
    if part == 0:
        y = lax.axis_index(Y)
        row = pl.multiple_of(place(y, outer) * 256, 256)
        qout_ref = qout_ref.at[pl.ds(row, 256), :]
    contract(part, outer, len_ref, u_ref, g_ref, mom_ref, seq_ref, qout_ref)


def group(part, outer, lengths, mine, other, pairs, mom, seqs, queries):
    seq_rows = 1 if part == 0 else SEQS
    carried, alias = [], {}
    if outer:
        carried = [mom, queries] if part == 0 else [mom, seqs, queries]
        alias = {5: 0, 6: 2} if part == 0 else {5: 0, 6: 1, 7: 2}
    return pl.pallas_call(
        functools.partial(group_kernel, part, outer),
        out_shape=(
            jax.ShapeDtypeStruct((COLS, HALF), jnp.float32),
            jax.ShapeDtypeStruct((seq_rows, COLS, HALF), jnp.float32),
            jax.ShapeDtypeStruct((QROWS, HALF), jnp.bfloat16),
        ),
        in_specs=[spec(SM)] + [spec(ANY)] * 4 + [spec(VM)] * len(carried),
        out_specs=(spec(VM),) * 3,
        scratch_shapes=[
            pltpu.VMEM((HALVES, 2 * ROWS, HALF), jnp.bfloat16),
            pltpu.VMEM((2, BLOCK, SEQ_LEN), jnp.bfloat16),
            pltpu.SemaphoreType.DMA((SEMS,)),
        ],
        input_output_aliases=alias,
        compiler_params=pltpu.CompilerParams(vmem_limit_bytes=16 << 20),
        cost_estimate=pl.CostEstimate(
            flops=4 * TOKENS * HALF * COLS // 4,
            bytes_accessed=6 << 20,
            transcendentals=0,
        ),
    )(lengths, mine, other, *pairs, *carried)


FAR = 2


def last_kernel(len_ref, scale_ref, mine_ref, other_ref, *refs):
    pairs, refs = (refs[0:2], refs[2:4]), refs[4:]
    moms, seq_a, seq_b, q_ins, refs = refs[0:2], refs[2:5], refs[5], refs[6:8], refs[8:]
    out_ref, score_ref, w_ref, s_ref, q_ref, u_ref, g_ref, qg_ref, p_ref, sem = refs
    y, _, _, _, c = where()
    copies = []
    for part in range(2):
        copies += group_copies(part, FAR, pairs[part], (mine_ref, other_ref), u_ref.at[part], g_ref.at[part], sem.at[part])
    for m, ref in enumerate((mine_ref, other_ref)):
        copies.append(pltpu.make_async_copy(ref.at[:, pl.ds(TOKENS, QROWS)], qg_ref.at[m], sem.at[2, m]))
    for copy in copies:
        copy.start()
    for part in range(2):
        w_ref[part] = moms[part][...]
        q_ref[part] = q_ins[part][...]
    for n, slot in enumerate((0, 1, 3)):
        s_ref[0, place(y, slot)] = seq_a[n][0]
    far = place(y, FAR)
    s_ref[0, far] = jnp.zeros((COLS, HALF), jnp.float32)
    s_ref[1] = seq_b[...]
    for copy in copies:
        copy.wait()
    row = pl.multiple_of(far * 256, 256)
    contract(0, FAR, len_ref, u_ref.at[0], g_ref.at[0], w_ref.at[0], s_ref.at[0, pl.ds(far, 1)], q_ref.at[0, pl.ds(row, 256), :])
    contract(1, FAR, len_ref, u_ref.at[1], g_ref.at[1], w_ref.at[1], s_ref.at[1], q_ref.at[1])

    mine_at = pl.multiple_of(c * BLOCK, BLOCK)
    other_at = pl.multiple_of((1 - c) * BLOCK, BLOCK)

    @pl.loop(0, FEAT // 256)
    def _(k):
        part, cols = k // 2, pl.ds(pl.multiple_of(lax.rem(k, 2) * 256, 256), 256)
        m = w_ref[part, :, cols] / scale_ref[SEQS]
        rows = pl.ds(pl.multiple_of(k * 256, 256), 256)
        out_ref[rows, pl.ds(mine_at, BLOCK)] = m[0:BLOCK, :].T
        out_ref[rows, pl.ds(other_at, BLOCK)] = m[BLOCK:COLS, :].T
        w_ref[part, :, cols] = 1.0 / (m + damping)

    @pl.loop(0, SEQS)
    def _(s):
        for part in range(2):
            p = w_ref[part] * s_ref[part, s] * scale_ref[s]
            p_ref[part] = p.astype(jnp.bfloat16)

        @pl.loop(0, 2)
        def _(k):
            rows = pl.ds(pl.multiple_of(k * 512, 512), 512)
            mapped = dot(p_ref[0], q_ref[0, rows, :], 1, 1)
            mapped += dot(p_ref[1], q_ref[1, rows, :], 1, 1)
            total = jnp.sum(mapped[0:BLOCK] * qg_ref[0, :, rows].astype(jnp.float32), axis=0, keepdims=True)
            total += jnp.sum(mapped[BLOCK:COLS] * qg_ref[1, :, rows].astype(jnp.float32), axis=0, keepdims=True)
            score_ref[pl.ds(s, 1), rows] = total


def last(lengths, scales, mine, other, pairs, carried):
    return pl.pallas_call(
        last_kernel,
        out_shape=(
            jax.ShapeDtypeStruct((FEAT, COLS), jnp.float32),
            jax.ShapeDtypeStruct((SEQS, QROWS), jnp.float32),
        ),
        in_specs=[spec(SM)] * 2 + [spec(ANY)] * 6 + [spec(VM)] * len(carried),
        out_specs=(spec(VM), spec(VM)),
        scratch_shapes=[
            pltpu.VMEM((2, COLS, HALF), jnp.float32),
            pltpu.VMEM((2, SEQS, COLS, HALF), jnp.float32),
            pltpu.VMEM((2, QROWS, HALF), jnp.bfloat16),
            pltpu.VMEM((2, HALVES, 2 * ROWS, HALF), jnp.bfloat16),
            pltpu.VMEM((2, 2, BLOCK, SEQ_LEN), jnp.bfloat16),
            pltpu.VMEM((2, BLOCK, QROWS), jnp.bfloat16),
            pltpu.VMEM((2, COLS, HALF), jnp.bfloat16),
            pltpu.SemaphoreType.DMA((3, SEMS)),
        ],
        compiler_params=pltpu.CompilerParams(vmem_limit_bytes=32 << 20),
        name="last",
    )(lengths, scales, mine, other, *pairs, *carried)


def shift(x, axis, step):
    return lax.ppermute(x, axis, [(i, (i + step) % RING) for i in range(RING)])


def spread(own, inner_axis, outer_axis, up):
    left = shift(own, inner_axis, 1)
    right = shift(own, inner_axis, -1)
    step, source = (1, left) if up else (-1, right)
    far = shift(source, inner_axis, step)
    pairs = (join(own, left), join(far, right))
    down = [shift(u, outer_axis, 1) for u in pairs]
    up = [shift(u, outer_axis, -1) for u in pairs]
    ends = (shift(down[0], outer_axis, 1), shift(up[1], outer_axis, -1))
    return [pairs, down, ends, up]


def at_z(k):
    k %= 2 * RING
    return k % RING * 2 + k // RING


def along_z(x, pairs):
    return lax.ppermute(x, (Z, H), [(at_z(a), at_z(b)) for a, b in pairs])


ONE = ((0, 1), (1, 2), (2, 3), (3, 4), (4, 7), (5, 0), (6, 5), (7, 6))
TWO = ((0, 5), (1, 6), (2, 7), (3, 0), (4, 3), (5, 4), (6, 1), (7, 2))
UP = tuple((k, k + 2) for k in range(8))
DOWN = tuple((k, k - 2) for k in range(8))


def local(act_in, grad_in, query_act, query_grad, act_basis, grad_basis, seq_lengths):
    own = rotate_act(seq_lengths, act_in, query_act, act_basis)
    blocks = [own] + [shift(own, Z, s) for s in range(1, RING)]

    packed = pack(grad_in, query_grad, own)
    received = lax.all_to_all(packed, (Y, X), 0, 0, tiled=True)
    odd, part = received[:, ROWS : 2 * ROWS], received[:, 2 * ROWS : SENT]
    parts = [received, along_z(odd, ONE), along_z(odd, TWO), along_z(part, UP), along_z(part, DOWN)]
    mine = rotate_grad(parts, grad_basis)
    other = lax.ppermute(mine, C, [(0, 1), (1, 0)])

    part_a, part_b = assemble(blocks)
    pairs = (spread(part_a, X, Y, True), spread(part_b, Y, X, False))
    moms, seqs, queries = [None, None], [[], []], [None, None]
    for outer in (0, 1, 3):
        for part in range(2):
            last_seqs = seqs[part][-1] if outer else None
            moms[part], s, queries[part] = group(part, outer, seq_lengths, mine, other, pairs[part][outer], moms[part], last_seqs, queries[part])
            seqs[part].append(s)

    counted = jnp.sum(seq_lengths).astype(jnp.float32)
    scales = jnp.concatenate(
        [lax.rsqrt(seq_lengths.astype(jnp.float32)), counted[None]]
    )
    carried = [*moms, *seqs[0], seqs[1][-1], *queries]
    far = [*pairs[0][FAR], *pairs[1][FAR]]
    moments, per_row = last(seq_lengths, scales, mine, other, far, carried)
    per_query = jnp.sum(per_row.reshape(SEQS, QUERIES, QUERY_LEN), axis=2)
    partial = per_query.reshape(2, 128) / math.sqrt(QUERY_LEN * D * FF)
    everywhere = jnp.broadcast_to(partial[None], (256, 2, 128))
    scores = lax.all_to_all(everywhere, ALL, 0, 0, tiled=True).sum(0)
    return moments, scores.reshape(SEQS, QUERIES).T


def solution(mesh):
    finer = Mesh(mesh.devices.reshape(4, 4, 4, 2, 2), ALL)
    placed = (P(DP, MP), P(DP, None), P(DP, MP), P(DP, None), P(MP, None), P(DP, None), P())

    return jax.shard_map(
        local, mesh=finer, in_specs=placed, out_specs=(P(MP, DP), P()), check_vma=False
    )
```

```python
import functools
import math

import jax
import jax.numpy as jnp
from jax import lax
from jax.experimental import pallas as pl
from jax.experimental.pallas import tpu as pltpu
from jax.sharding import Mesh
from jax.sharding import PartitionSpec as P

D = 4096
FF = 16384
BLOCK = 128
SEQS = 4
SEQ_LEN = 2048
TOKENS = 8192
QUERIES = 64
QUERY_LEN = 16
QROWS = 1024
RING = 4
TOK = 128
QTOK = 16
ROWS = TOK + QTOK
FEAT = 1024
HALF = 512
COLS = 256
UNIT = 512
KC = 256
PLANE = 16
Y, X, Z, H, C = "dp_0", "dp_1", "dp_2", "mp_0", "mp_1"
DP = (Y, X, Z)
MP = (H, C)
ALL = (Y, X, Z, H, C)
damping = 0.1


VM = pltpu.VMEM
SM = pltpu.SMEM
ANY = pl.ANY


def spec(space):
    return pl.BlockSpec(memory_space=space)


def dot(a, b, da, db):
    return lax.dot_general(
        a, b, (((da,), (db,)), ((), ())), preferred_element_type=jnp.float32
    )


def where():
    return tuple(lax.axis_index(a) for a in (Y, X, Z, H, C))


def rotate_act_kernel(len_ref, act_ref, q_ref, basis_ref, out_ref):
    y, x, z, _, _ = where()
    live = jnp.clip(len_ref[y] - (x * RING + z) * TOK, 0, TOK)
    mask = lax.broadcasted_iota(jnp.int32, (TOK, BLOCK), 0) < live
    for b in range(FEAT // BLOCK):
        cols = pl.ds(b * BLOCK, BLOCK)
        basis = basis_ref[cols, :]
        t = dot(act_ref[:, cols], basis, 1, 0)
        out_ref[0:TOK, cols] = jnp.where(mask, t, 0.0).astype(jnp.bfloat16)
        q = dot(q_ref[:, cols], basis, 1, 0)
        out_ref[TOK:ROWS, cols] = q.astype(jnp.bfloat16)


def rotate_act(lengths, act_in, query_act, act_basis):
    return pl.pallas_call(
        rotate_act_kernel,
        out_shape=jax.ShapeDtypeStruct((ROWS, FEAT), jnp.bfloat16),
        in_specs=[spec(SM), spec(VM), spec(VM), spec(VM)],
        out_specs=spec(VM),
        name="rotate_act",
    )(lengths, act_in, query_act, act_basis)


PART = ROWS // 2
SENT = 2 * ROWS + PART


def pack_kernel(g_ref, q_ref, after_ref, out_ref, sem):
    _, _, z, h, c = where()
    copies = []

    def send(src, dst):
        copies.append(pltpu.make_async_copy(src, dst, sem.at[len(copies)]))

    for n in range(PLANE):

        def cols(step):
            at = n * RING * COLS + lax.rem(z + step, RING) * COLS + c * BLOCK
            return pl.ds(pl.multiple_of(at, BLOCK), BLOCK)

        odd = cols(1 + 2 * h)
        send(g_ref.at[:, cols(0)], out_ref.at[n, pl.ds(0, TOK), :])
        send(q_ref.at[:, cols(0)], out_ref.at[n, pl.ds(TOK, QTOK), :])
        send(g_ref.at[:, odd], out_ref.at[n, pl.ds(ROWS, TOK), :])
        send(q_ref.at[:, odd], out_ref.at[n, pl.ds(ROWS + TOK, QTOK), :])
    for copy in copies:
        copy.start()

    def half(n, pieces):
        at = n * RING * COLS + lax.rem(z + 2, RING) * COLS + c * BLOCK
        cols = pl.ds(pl.multiple_of(at, BLOCK), BLOCK)
        return [
            pltpu.make_async_copy(
                ref.at[rows, cols], out_ref.at[n, to, :], sem.at[4 * PLANE + 2 * n + k]
            )
            for k, (ref, rows, to) in enumerate(pieces)
        ]

    cut = 2 * ROWS + TOK - PART
    halves = (
        ((g_ref, pl.ds(0, PART), pl.ds(2 * ROWS, PART)),),
        (
            (g_ref, pl.ds(PART, TOK - PART), pl.ds(2 * ROWS, TOK - PART)),
            (q_ref, pl.ds(0, QTOK), pl.ds(cut, QTOK)),
        ),
    )
    for k in range(2):

        @pl.when(h == k)
        def _():
            rest = [copy for n in range(PLANE) for copy in half(n, halves[k])]
            for copy in rest:
                copy.start()
            for copy in rest:
                copy.wait()

    for copy in copies:
        copy.wait()


def pack(grad_in, query_grad, after):
    return pl.pallas_call(
        pack_kernel,
        out_shape=jax.ShapeDtypeStruct((PLANE, SENT, BLOCK), jnp.bfloat16),
        in_specs=[spec(ANY)] * 3,
        out_specs=spec(VM),
        scratch_shapes=[pltpu.SemaphoreType.DMA((6 * PLANE,))],
        name="pack",
    )(grad_in, query_grad, after)


def rotate_grad_kernel(own_ref, u1_ref, u2_ref, f1_ref, f2_ref, basis_ref, out_ref, q_ref, far_ref):
    _, _, z, h, c = where()
    at = pl.multiple_of(c * BLOCK, BLOCK)
    basis_t = basis_ref[pl.ds(at, BLOCK), :].astype(jnp.float32).T.astype(jnp.bfloat16)
    p = h * RING + z
    first = jnp.logical_and(p >= 2, p < 6)

    @pl.when(first)
    def _():
        far_ref[:, 0:PART, :] = f1_ref[...]
        far_ref[:, PART:ROWS, :] = f2_ref[...]

    @pl.when(jnp.logical_not(first))
    def _():
        far_ref[:, 0:PART, :] = f2_ref[...]
        far_ref[:, PART:ROWS, :] = f1_ref[...]

    below = jnp.logical_and(p >= 1, p < 5)
    step = jnp.where(below, 3, 1)
    group = 4
    for ref, s in ((own_ref, 0), (u1_ref, step), (u2_ref, RING - step), (far_ref, 2)):
        src = lax.rem(z + s, RING)

        @pl.loop(0, PLANE // group)
        def _(i):
            rows = ref[pl.ds(i * group, group), 0:TOK, :].reshape(group * TOK, BLOCK)
            t = dot(basis_t, rows, 1, 1).astype(jnp.bfloat16)
            for k in range(group):
                block = (i * group + k) * RING + src
                at = pl.multiple_of(block * TOK, TOK)
                out_ref[:, pl.ds(at, TOK)] = t[:, k * TOK : (k + 1) * TOK]
                at = pl.multiple_of(block * QTOK, QTOK)
                q_ref[pl.ds(at, QTOK), :] = ref[i * group + k, TOK:ROWS, :]

    q = dot(basis_t, q_ref[...], 1, 1)
    out_ref[:, pl.ds(TOKENS, QROWS)] = q.astype(jnp.bfloat16)


def rotate_grad(parts, basis):
    return pl.pallas_call(
        rotate_grad_kernel,
        out_shape=jax.ShapeDtypeStruct((BLOCK, TOKENS + QROWS), jnp.bfloat16),
        in_specs=[spec(VM)] * 6,
        out_specs=spec(VM),
        scratch_shapes=[
            pltpu.VMEM((QROWS, BLOCK), jnp.bfloat16),
            pltpu.VMEM((PLANE, ROWS, BLOCK), jnp.bfloat16),
        ],
        compiler_params=pltpu.CompilerParams(vmem_limit_bytes=16 << 20),
        cost_estimate=pl.CostEstimate(
            flops=2 * (TOKENS + QROWS) * BLOCK * BLOCK,
            bytes_accessed=5 << 20,
            transcendentals=0,
        ),
        name="rotate_grad",
    )(*parts, basis)


def assemble_kernel(*refs):
    ins, outs = refs[:RING], refs[RING:]
    z = lax.axis_index(Z)
    for slot in range(RING):
        zb = lax.rem(z - slot + RING, RING)
        half, odd = zb // 2, lax.rem(zb, 2)
        at = pl.multiple_of(odd * TOK, TOK)
        qat = pl.multiple_of(2 * TOK + odd * QTOK, QTOK)
        for part in range(2):
            cols = pl.ds(part * HALF, HALF)
            outs[part][half, pl.ds(at, TOK), :] = ins[slot][0:TOK, cols]
            outs[part][half, pl.ds(qat, QTOK), :] = ins[slot][TOK:ROWS, cols]


def assemble(blocks):
    unit = jax.ShapeDtypeStruct((2, 2 * ROWS, HALF), jnp.bfloat16)
    return pl.pallas_call(
        assemble_kernel,
        out_shape=(unit, unit),
        in_specs=[spec(VM)] * RING,
        out_specs=(spec(VM), spec(VM)),
        compiler_params=pltpu.CompilerParams(vmem_limit_bytes=8 << 20),
        name="assemble",
    )(*blocks)


def join_kernel(*refs):
    ins, out_ref, sem = refs[:-2], refs[-2], refs[-1]
    copies, at = [], 0
    for n, ref in enumerate(ins):
        size = ref.shape[0]
        copies.append(pltpu.make_async_copy(ref, out_ref.at[pl.ds(at, size)], sem.at[n]))
        at += size
    for c in copies:
        c.start()
    for c in copies:
        c.wait()


def join(*pieces):
    return pl.pallas_call(
        join_kernel,
        out_shape=jax.ShapeDtypeStruct((4, 2 * ROWS, HALF), jnp.bfloat16),
        in_specs=[spec(ANY)] * len(pieces),
        out_specs=spec(VM),
        scratch_shapes=[pltpu.SemaphoreType.DMA((len(pieces),))],
        compiler_params=pltpu.CompilerParams(vmem_limit_bytes=4 << 20),
        name="join",
    )(*pieces)


def place(at, slot):
    return lax.rem(at - slot + RING, RING)


HALVES = 2 * RING


def group_copies(part, outer, pair_refs, grad_refs, u_ref, g_ref, sem):
    y, x, _, _, _ = where()
    out = [
        pltpu.make_async_copy(ref, u_ref.at[pl.ds(4 * n, 4)], sem.at[n])
        for n, ref in enumerate(pair_refs)
    ]
    for m, ref in enumerate(grad_refs):
        if part == 0:
            at = pl.multiple_of(place(y, outer) * SEQ_LEN, SEQ_LEN)
            out.append(pltpu.make_async_copy(ref.at[:, pl.ds(at, SEQ_LEN)], g_ref.at[m], sem.at[2 + RING * m]))
            continue
        for s in range(SEQS):
            at = pl.multiple_of(s * SEQ_LEN + place(x, outer) * UNIT, UNIT)
            out.append(pltpu.make_async_copy(ref.at[:, pl.ds(at, UNIT)], g_ref.at[m, :, pl.ds(s * UNIT, UNIT)], sem.at[2 + RING * m + s]))
    return out


SEMS = 2 + 2 * RING


def contract(part, outer, pair, len_ref, u_ref, g_ref, mom_ref, seq_ref, q_ref):
    y, x, _, _, _ = where()

    @pl.loop(pair * RING, (pair + 1) * RING)
    def _(n):
        v = place(x if part == 0 else y, n // 2)
        half = lax.rem(n, 2)
        seq, block = (place(y, outer), v) if part == 0 else (v, place(x, outer))
        q_at = v * 64 if part == 0 else v * 256 + block * 64
        q_at = pl.multiple_of(q_at + half * 32, 32)
        q_ref[pl.ds(q_at, 32), :] = u_ref[n, KC : KC + 32, :]

        @pl.when(len_ref[seq] > block * UNIT + half * KC)
        def _():
            at = pl.multiple_of(v * UNIT + half * KC, KC)
            a = u_ref[n, 0:KC, :]
            g = jnp.concatenate([g_ref[0, :, pl.ds(at, KC)], g_ref[1, :, pl.ds(at, KC)]])
            seq_ref[seq if part else 0] += dot(g, a, 1, 0)
            mom_ref[...] += dot(g * g, a * a, 1, 0)


def group_kernel(part, outer, len_ref, mine_ref, other_ref, p_ref, q_ref, *refs):
    carried = 0 if outer == 0 else 2 if part == 0 else 3
    refs = refs[carried:]
    mom_ref, seq_ref, qout_ref, u_ref, g_ref, sem = refs
    copies = group_copies(part, outer, (p_ref, q_ref), (mine_ref, other_ref), u_ref, g_ref, sem)
    for c in (*copies[2:], *copies[:2]):
        c.start()
    if not outer:
        mom_ref[...] = jnp.zeros_like(mom_ref)
    if not (outer and part):
        seq_ref[...] = jnp.zeros_like(seq_ref)
    if part == 0:
        y = lax.axis_index(Y)
        row = pl.multiple_of(place(y, outer) * 256, 256)
        qout_ref = qout_ref.at[pl.ds(row, 256), :]
    for c in copies[2:]:
        c.wait()
    for pair in range(2):
        copies[pair].wait()
        contract(part, outer, pair, len_ref, u_ref, g_ref, mom_ref, seq_ref, qout_ref)


def group(part, outer, lengths, mine, other, pairs, mom, seqs, queries):
    seq_rows = 1 if part == 0 else SEQS
    carried, alias = [], {}
    if outer:
        carried = [mom, queries] if part == 0 else [mom, seqs, queries]
        alias = {5: 0, 6: 2} if part == 0 else {5: 0, 6: 1, 7: 2}
    return pl.pallas_call(
        functools.partial(group_kernel, part, outer),
        out_shape=(
            jax.ShapeDtypeStruct((COLS, HALF), jnp.float32),
            jax.ShapeDtypeStruct((seq_rows, COLS, HALF), jnp.float32),
            jax.ShapeDtypeStruct((QROWS, HALF), jnp.bfloat16),
        ),
        in_specs=[spec(SM)] + [spec(ANY)] * 4 + [spec(VM)] * len(carried),
        out_specs=(spec(VM),) * 3,
        scratch_shapes=[
            pltpu.VMEM((HALVES, 2 * ROWS, HALF), jnp.bfloat16),
            pltpu.VMEM((2, BLOCK, SEQ_LEN), jnp.bfloat16),
            pltpu.SemaphoreType.DMA((SEMS,)),
        ],
        input_output_aliases=alias,
        compiler_params=pltpu.CompilerParams(vmem_limit_bytes=16 << 20),
        cost_estimate=pl.CostEstimate(
            flops=4 * TOKENS * HALF * COLS // 4,
            bytes_accessed=6 << 20,
            transcendentals=0,
        ),
    )(lengths, mine, other, *pairs, *carried)


FAR = 2


def last_kernel(len_ref, scale_ref, mine_ref, other_ref, *refs):
    pairs, refs = (refs[0:2], refs[2:4]), refs[4:]
    moms, seq_a, seq_b, q_ins, refs = refs[0:2], refs[2:5], refs[5], refs[6:8], refs[8:]
    out_ref, score_ref, w_ref, s_ref, q_ref, u_ref, g_ref, qg_ref, p_ref, sem = refs
    y, _, _, _, c = where()
    copies = [
        group_copies(part, FAR, pairs[part], (mine_ref, other_ref), u_ref.at[part], g_ref.at[part], sem.at[part])
        for part in range(2)
    ]
    copies.append([pltpu.make_async_copy(ref.at[:, pl.ds(TOKENS, QROWS)], qg_ref.at[m], sem.at[2, m]) for m, ref in enumerate((mine_ref, other_ref))])
    for some in copies:
        for copy in (*some[2:], *some[:2]):
            copy.start()
    for part in range(2):
        w_ref[part] = moms[part][...]
        q_ref[part] = q_ins[part][...]
    for n, slot in enumerate((0, 1, 3)):
        s_ref[0, place(y, slot)] = seq_a[n][0]
    far = place(y, FAR)
    s_ref[0, far] = jnp.zeros((COLS, HALF), jnp.float32)
    s_ref[1] = seq_b[...]
    row = pl.multiple_of(far * 256, 256)
    seq_refs = s_ref.at[0, pl.ds(far, 1)], s_ref.at[1]
    q_refs = q_ref.at[0, pl.ds(row, 256), :], q_ref.at[1]
    for part in range(2):
        for copy in copies[part][2:]:
            copy.wait()
        for pair in range(2):
            copies[part][pair].wait()
            contract(part, FAR, pair, len_ref, u_ref.at[part], g_ref.at[part], w_ref.at[part], seq_refs[part], q_refs[part])
    for copy in copies[2]:
        copy.wait()

    mine_at = pl.multiple_of(c * BLOCK, BLOCK)
    other_at = pl.multiple_of((1 - c) * BLOCK, BLOCK)

    @pl.loop(0, FEAT // 256)
    def _(k):
        part, cols = k // 2, pl.ds(pl.multiple_of(lax.rem(k, 2) * 256, 256), 256)
        m = w_ref[part, :, cols] / scale_ref[SEQS]
        rows = pl.ds(pl.multiple_of(k * 256, 256), 256)
        out_ref[rows, pl.ds(mine_at, BLOCK)] = m[0:BLOCK, :].T
        out_ref[rows, pl.ds(other_at, BLOCK)] = m[BLOCK:COLS, :].T
        w_ref[part, :, cols] = 1.0 / (m + damping)

    @pl.loop(0, SEQS)
    def _(s):
        for part in range(2):
            p = w_ref[part] * s_ref[part, s] * scale_ref[s]
            p_ref[part] = p.astype(jnp.bfloat16)

        @pl.loop(0, 2)
        def _(k):
            rows = pl.ds(pl.multiple_of(k * 512, 512), 512)
            mapped = dot(p_ref[0], q_ref[0, rows, :], 1, 1)
            mapped += dot(p_ref[1], q_ref[1, rows, :], 1, 1)
            total = jnp.sum(mapped[0:BLOCK] * qg_ref[0, :, rows].astype(jnp.float32), axis=0, keepdims=True)
            total += jnp.sum(mapped[BLOCK:COLS] * qg_ref[1, :, rows].astype(jnp.float32), axis=0, keepdims=True)
            score_ref[pl.ds(s, 1), rows] = total


def last(lengths, scales, mine, other, pairs, carried):
    return pl.pallas_call(
        last_kernel,
        out_shape=(
            jax.ShapeDtypeStruct((FEAT, COLS), jnp.float32),
            jax.ShapeDtypeStruct((SEQS, QROWS), jnp.float32),
        ),
        in_specs=[spec(SM)] * 2 + [spec(ANY)] * 6 + [spec(VM)] * len(carried),
        out_specs=(spec(VM), spec(VM)),
        scratch_shapes=[
            pltpu.VMEM((2, COLS, HALF), jnp.float32),
            pltpu.VMEM((2, SEQS, COLS, HALF), jnp.float32),
            pltpu.VMEM((2, QROWS, HALF), jnp.bfloat16),
            pltpu.VMEM((2, HALVES, 2 * ROWS, HALF), jnp.bfloat16),
            pltpu.VMEM((2, 2, BLOCK, SEQ_LEN), jnp.bfloat16),
            pltpu.VMEM((2, BLOCK, QROWS), jnp.bfloat16),
            pltpu.VMEM((2, COLS, HALF), jnp.bfloat16),
            pltpu.SemaphoreType.DMA((3, SEMS)),
        ],
        compiler_params=pltpu.CompilerParams(vmem_limit_bytes=32 << 20),
        name="last",
    )(lengths, scales, mine, other, *pairs, *carried)


def shift(x, axis, step):
    return lax.ppermute(x, axis, [(i, (i + step) % RING) for i in range(RING)])


def spread(own, inner_axis, outer_axis, up):
    left = shift(own, inner_axis, 1)
    right = shift(own, inner_axis, -1)
    step, source = (1, left) if up else (-1, right)
    far = shift(source, inner_axis, step)
    pairs = (join(own, left), join(far, right))
    down = [shift(u, outer_axis, 1) for u in pairs]
    up = [shift(u, outer_axis, -1) for u in pairs]
    ends = (shift(down[0], outer_axis, 1), shift(up[1], outer_axis, -1))
    return [pairs, down, ends, up]


def at_z(k):
    k %= 2 * RING
    return k % RING * 2 + k // RING


def along_z(x, pairs):
    return lax.ppermute(x, (Z, H), [(at_z(a), at_z(b)) for a, b in pairs])


ONE = ((0, 1), (1, 2), (2, 3), (3, 4), (4, 7), (5, 0), (6, 5), (7, 6))
TWO = ((0, 5), (1, 6), (2, 7), (3, 0), (4, 3), (5, 4), (6, 1), (7, 2))
UP = tuple((k, k + 2) for k in range(8))
DOWN = tuple((k, k - 2) for k in range(8))


def local(act_in, grad_in, query_act, query_grad, act_basis, grad_basis, seq_lengths):
    own = rotate_act(seq_lengths, act_in, query_act, act_basis)
    blocks = [own] + [shift(own, Z, s) for s in range(1, RING)]

    packed = pack(grad_in, query_grad, own)
    received = lax.all_to_all(packed, (Y, X), 0, 0, tiled=True)
    odd, part = received[:, ROWS : 2 * ROWS], received[:, 2 * ROWS : SENT]
    parts = [received, along_z(odd, ONE), along_z(odd, TWO), along_z(part, UP), along_z(part, DOWN)]
    mine = rotate_grad(parts, grad_basis)
    other = lax.ppermute(mine, C, [(0, 1), (1, 0)])

    part_a, part_b = assemble(blocks)
    pairs = (spread(part_a, X, Y, True), spread(part_b, Y, X, False))
    moms, seqs, queries = [None, None], [[], []], [None, None]
    for outer in (0, 1, 3):
        for part in range(2):
            last_seqs = seqs[part][-1] if outer else None
            moms[part], s, queries[part] = group(part, outer, seq_lengths, mine, other, pairs[part][outer], moms[part], last_seqs, queries[part])
            seqs[part].append(s)

    counted = jnp.sum(seq_lengths).astype(jnp.float32)
    scales = jnp.concatenate(
        [lax.rsqrt(seq_lengths.astype(jnp.float32)), counted[None]]
    )
    carried = [*moms, *seqs[0], seqs[1][-1], *queries]
    far = [*pairs[0][FAR], *pairs[1][FAR]]
    moments, per_row = last(seq_lengths, scales, mine, other, far, carried)
    per_query = jnp.sum(per_row.reshape(SEQS, QUERIES, QUERY_LEN), axis=2)
    partial = per_query.reshape(2, 128) / math.sqrt(QUERY_LEN * D * FF)
    partial += lax.ppermute(partial, C, [(0, 1), (1, 0)])
    everywhere = jnp.broadcast_to(partial[None], (128, 2, 128))
    scores = lax.all_to_all(everywhere, (Y, X, Z, H), 0, 0, tiled=True).sum(0)
    return moments, scores.reshape(SEQS, QUERIES).T


def solution(mesh):
    finer = Mesh(mesh.devices.reshape(4, 4, 4, 2, 2), ALL)
    placed = (P(DP, MP), P(DP, None), P(DP, MP), P(DP, None), P(MP, None), P(DP, None), P())

    return jax.shard_map(
        local, mesh=finer, in_specs=placed, out_specs=(P(MP, DP), P()), check_vma=False
    )
```

```python
import functools
import math

import jax
import jax.numpy as jnp
from jax import lax
from jax.experimental import pallas as pl
from jax.experimental.pallas import tpu as pltpu
from jax.sharding import Mesh
from jax.sharding import PartitionSpec as P

D = 4096
FF = 16384
BLOCK = 128
SEQS = 4
SEQ_LEN = 2048
TOKENS = 8192
QUERIES = 64
QUERY_LEN = 16
QROWS = 1024
RING = 4
TOK = 128
QTOK = 16
ROWS = TOK + QTOK
FEAT = 1024
HALF = 512
COLS = 256
UNIT = 512
KC = 256
PLANE = 16
Y, X, Z, H, C = "dp_0", "dp_1", "dp_2", "mp_0", "mp_1"
DP = (Y, X, Z)
MP = (H, C)
ALL = (Y, X, Z, H, C)
damping = 0.1


VM = pltpu.VMEM
SM = pltpu.SMEM
ANY = pl.ANY


def spec(space):
    return pl.BlockSpec(memory_space=space)


def dot(a, b, da, db):
    return lax.dot_general(
        a, b, (((da,), (db,)), ((), ())), preferred_element_type=jnp.float32
    )


def where():
    return tuple(lax.axis_index(a) for a in (Y, X, Z, H, C))


def rotate_act_kernel(len_ref, act_ref, q_ref, basis_ref, out_ref):
    y, x, z, _, _ = where()
    live = jnp.clip(len_ref[y] - (x * RING + z) * TOK, 0, TOK)
    mask = lax.broadcasted_iota(jnp.int32, (TOK, BLOCK), 0) < live
    for b in range(FEAT // BLOCK):
        cols = pl.ds(b * BLOCK, BLOCK)
        basis = basis_ref[cols, :]
        t = dot(act_ref[:, cols], basis, 1, 0)
        out_ref[0:TOK, cols] = jnp.where(mask, t, 0.0).astype(jnp.bfloat16)
        q = dot(q_ref[:, cols], basis, 1, 0)
        out_ref[TOK:ROWS, cols] = q.astype(jnp.bfloat16)


def rotate_act(lengths, act_in, query_act, act_basis):
    return pl.pallas_call(
        rotate_act_kernel,
        out_shape=jax.ShapeDtypeStruct((ROWS, FEAT), jnp.bfloat16),
        in_specs=[spec(SM), spec(VM), spec(VM), spec(VM)],
        out_specs=spec(VM),
        name="rotate_act",
    )(lengths, act_in, query_act, act_basis)


PART = ROWS // 2
SENT = 2 * ROWS + PART


def pack_kernel(g_ref, q_ref, after_ref, out_ref, sem):
    _, _, z, h, c = where()
    copies = []

    def send(src, dst):
        copies.append(pltpu.make_async_copy(src, dst, sem.at[len(copies)]))

    for n in range(PLANE):

        def cols(step):
            at = n * RING * COLS + lax.rem(z + step, RING) * COLS + c * BLOCK
            return pl.ds(pl.multiple_of(at, BLOCK), BLOCK)

        odd = cols(1 + 2 * h)
        send(g_ref.at[:, cols(0)], out_ref.at[n, pl.ds(0, TOK), :])
        send(q_ref.at[:, cols(0)], out_ref.at[n, pl.ds(TOK, QTOK), :])
        send(g_ref.at[:, odd], out_ref.at[n, pl.ds(ROWS, TOK), :])
        send(q_ref.at[:, odd], out_ref.at[n, pl.ds(ROWS + TOK, QTOK), :])
    for copy in copies:
        copy.start()

    def half(n, pieces):
        at = n * RING * COLS + lax.rem(z + 2, RING) * COLS + c * BLOCK
        cols = pl.ds(pl.multiple_of(at, BLOCK), BLOCK)
        return [
            pltpu.make_async_copy(
                ref.at[rows, cols], out_ref.at[n, to, :], sem.at[4 * PLANE + 2 * n + k]
            )
            for k, (ref, rows, to) in enumerate(pieces)
        ]

    cut = 2 * ROWS + TOK - PART
    halves = (
        ((g_ref, pl.ds(0, PART), pl.ds(2 * ROWS, PART)),),
        (
            (g_ref, pl.ds(PART, TOK - PART), pl.ds(2 * ROWS, TOK - PART)),
            (q_ref, pl.ds(0, QTOK), pl.ds(cut, QTOK)),
        ),
    )
    for k in range(2):

        @pl.when(h == k)
        def _():
            rest = [copy for n in range(PLANE) for copy in half(n, halves[k])]
            for copy in rest:
                copy.start()
            for copy in rest:
                copy.wait()

    for copy in copies:
        copy.wait()


def pack(grad_in, query_grad, after):
    return pl.pallas_call(
        pack_kernel,
        out_shape=jax.ShapeDtypeStruct((PLANE, SENT, BLOCK), jnp.bfloat16),
        in_specs=[spec(ANY)] * 3,
        out_specs=spec(VM),
        scratch_shapes=[pltpu.SemaphoreType.DMA((6 * PLANE,))],
        name="pack",
    )(grad_in, query_grad, after)


def rotate_grad_kernel(own_ref, u1_ref, u2_ref, f1_ref, f2_ref, basis_ref, out_ref, q_ref, far_ref):
    _, _, z, h, c = where()
    at = pl.multiple_of(c * BLOCK, BLOCK)
    basis_t = basis_ref[pl.ds(at, BLOCK), :].astype(jnp.float32).T.astype(jnp.bfloat16)
    p = h * RING + z
    first = jnp.logical_and(p >= 2, p < 6)

    @pl.when(first)
    def _():
        far_ref[:, 0:PART, :] = f1_ref[...]
        far_ref[:, PART:ROWS, :] = f2_ref[...]

    @pl.when(jnp.logical_not(first))
    def _():
        far_ref[:, 0:PART, :] = f2_ref[...]
        far_ref[:, PART:ROWS, :] = f1_ref[...]

    below = jnp.logical_and(p >= 1, p < 5)
    step = jnp.where(below, 3, 1)
    group = 4
    for ref, s in ((own_ref, 0), (u1_ref, step), (u2_ref, RING - step), (far_ref, 2)):
        src = lax.rem(z + s, RING)

        @pl.loop(0, PLANE // group)
        def _(i):
            rows = ref[pl.ds(i * group, group), 0:TOK, :].reshape(group * TOK, BLOCK)
            t = dot(basis_t, rows, 1, 1).astype(jnp.bfloat16)
            for k in range(group):
                block = (i * group + k) * RING + src
                at = pl.multiple_of(block * TOK, TOK)
                out_ref[:, pl.ds(at, TOK)] = t[:, k * TOK : (k + 1) * TOK]
                at = pl.multiple_of(block * QTOK, QTOK)
                q_ref[pl.ds(at, QTOK), :] = ref[i * group + k, TOK:ROWS, :]

    q = dot(basis_t, q_ref[...], 1, 1)
    out_ref[:, pl.ds(TOKENS, QROWS)] = q.astype(jnp.bfloat16)


def rotate_grad(parts, basis):
    return pl.pallas_call(
        rotate_grad_kernel,
        out_shape=jax.ShapeDtypeStruct((BLOCK, TOKENS + QROWS), jnp.bfloat16),
        in_specs=[spec(VM)] * 6,
        out_specs=spec(VM),
        scratch_shapes=[
            pltpu.VMEM((QROWS, BLOCK), jnp.bfloat16),
            pltpu.VMEM((PLANE, ROWS, BLOCK), jnp.bfloat16),
        ],
        compiler_params=pltpu.CompilerParams(vmem_limit_bytes=16 << 20),
        cost_estimate=pl.CostEstimate(
            flops=2 * (TOKENS + QROWS) * BLOCK * BLOCK,
            bytes_accessed=5 << 20,
            transcendentals=0,
        ),
        name="rotate_grad",
    )(*parts, basis)


def assemble_kernel(*refs):
    ins, outs = refs[:RING], refs[RING:]
    z = lax.axis_index(Z)
    for slot in range(RING):
        zb = lax.rem(z - slot + RING, RING)
        half, odd = zb // 2, lax.rem(zb, 2)
        at = pl.multiple_of(odd * TOK, TOK)
        qat = pl.multiple_of(2 * TOK + odd * QTOK, QTOK)
        for part in range(2):
            cols = pl.ds(part * HALF, HALF)
            outs[part][half, pl.ds(at, TOK), :] = ins[slot][0:TOK, cols]
            outs[part][half, pl.ds(qat, QTOK), :] = ins[slot][TOK:ROWS, cols]


def assemble(blocks):
    unit = jax.ShapeDtypeStruct((2, 2 * ROWS, HALF), jnp.bfloat16)
    return pl.pallas_call(
        assemble_kernel,
        out_shape=(unit, unit),
        in_specs=[spec(VM)] * RING,
        out_specs=(spec(VM), spec(VM)),
        compiler_params=pltpu.CompilerParams(vmem_limit_bytes=8 << 20),
        name="assemble",
    )(*blocks)


def join_kernel(*refs):
    ins, out_ref, sem = refs[:-2], refs[-2], refs[-1]
    copies, at = [], 0
    for n, ref in enumerate(ins):
        size = ref.shape[0]
        copies.append(pltpu.make_async_copy(ref, out_ref.at[pl.ds(at, size)], sem.at[n]))
        at += size
    for c in copies:
        c.start()
    for c in copies:
        c.wait()


def join(*pieces):
    return pl.pallas_call(
        join_kernel,
        out_shape=jax.ShapeDtypeStruct((4, 2 * ROWS, HALF), jnp.bfloat16),
        in_specs=[spec(ANY)] * len(pieces),
        out_specs=spec(VM),
        scratch_shapes=[pltpu.SemaphoreType.DMA((len(pieces),))],
        compiler_params=pltpu.CompilerParams(vmem_limit_bytes=4 << 20),
        name="join",
    )(*pieces)


def place(at, slot):
    return lax.rem(at - slot + RING, RING)


HALVES = 2 * RING


def group_copies(part, outer, pair_refs, grad_refs, u_ref, g_ref, sem):
    y, x, _, _, _ = where()
    out = [
        pltpu.make_async_copy(ref, u_ref.at[pl.ds(4 * n, 4)], sem.at[n])
        for n, ref in enumerate(pair_refs)
    ]
    for m, ref in enumerate(grad_refs):
        if part == 0:
            at = pl.multiple_of(place(y, outer) * SEQ_LEN, SEQ_LEN)
            out.append(pltpu.make_async_copy(ref.at[:, pl.ds(at, SEQ_LEN)], g_ref.at[m], sem.at[2 + RING * m]))
            continue
        for s in range(SEQS):
            at = pl.multiple_of(s * SEQ_LEN + place(x, outer) * UNIT, UNIT)
            out.append(pltpu.make_async_copy(ref.at[:, pl.ds(at, UNIT)], g_ref.at[m, :, pl.ds(s * UNIT, UNIT)], sem.at[2 + RING * m + s]))
    return out


SEMS = 2 + 2 * RING


def contract(part, outer, pair, len_ref, u_ref, g_ref, mom_ref, seq_ref, q_ref):
    y, x, _, _, _ = where()

    @pl.loop(pair * RING, (pair + 1) * RING)
    def _(n):
        v = place(x if part == 0 else y, n // 2)
        half = lax.rem(n, 2)
        seq, block = (place(y, outer), v) if part == 0 else (v, place(x, outer))
        q_at = v * 64 if part == 0 else v * 256 + block * 64
        q_at = pl.multiple_of(q_at + half * 32, 32)
        q_ref[pl.ds(q_at, 32), :] = u_ref[n, KC : KC + 32, :]

        @pl.when(len_ref[seq] > block * UNIT + half * KC)
        def _():
            at = pl.multiple_of(v * UNIT + half * KC, KC)
            a = u_ref[n, 0:KC, :]
            g = jnp.concatenate([g_ref[0, :, pl.ds(at, KC)], g_ref[1, :, pl.ds(at, KC)]])
            seq_ref[seq if part else 0] += dot(g, a, 1, 0)
            mom_ref[...] += dot(g * g, a * a, 1, 0)


def group_kernel(part, outer, len_ref, mine_ref, other_ref, p_ref, q_ref, *refs):
    carried = 0 if outer == 0 else 2 if part == 0 else 3
    refs = refs[carried:]
    mom_ref, seq_ref, qout_ref, u_ref, g_ref, sem = refs
    copies = group_copies(part, outer, (p_ref, q_ref), (mine_ref, other_ref), u_ref, g_ref, sem)
    for c in (*copies[2:], *copies[:2]):
        c.start()
    if not outer:
        mom_ref[...] = jnp.zeros_like(mom_ref)
    if not (outer and part):
        seq_ref[...] = jnp.zeros_like(seq_ref)
    if part == 0:
        y = lax.axis_index(Y)
        row = pl.multiple_of(place(y, outer) * 256, 256)
        qout_ref = qout_ref.at[pl.ds(row, 256), :]
    for c in copies[2:]:
        c.wait()
    for pair in range(2):
        copies[pair].wait()
        contract(part, outer, pair, len_ref, u_ref, g_ref, mom_ref, seq_ref, qout_ref)


def group(part, outer, lengths, mine, other, pairs, mom, seqs, queries):
    seq_rows = 1 if part == 0 else SEQS
    carried, alias = [], {}
    if outer:
        carried = [mom, queries] if part == 0 else [mom, seqs, queries]
        alias = {5: 0, 6: 2} if part == 0 else {5: 0, 6: 1, 7: 2}
    return pl.pallas_call(
        functools.partial(group_kernel, part, outer),
        out_shape=(
            jax.ShapeDtypeStruct((COLS, HALF), jnp.float32),
            jax.ShapeDtypeStruct((seq_rows, COLS, HALF), jnp.float32),
            jax.ShapeDtypeStruct((QROWS, HALF), jnp.bfloat16),
        ),
        in_specs=[spec(SM)] + [spec(pltpu.HBM)] * 2 + [spec(ANY)] * 2 + [spec(VM)] * len(carried),
        out_specs=(spec(VM),) * 3,
        scratch_shapes=[
            pltpu.VMEM((HALVES, 2 * ROWS, HALF), jnp.bfloat16),
            pltpu.VMEM((2, BLOCK, SEQ_LEN), jnp.bfloat16),
            pltpu.SemaphoreType.DMA((SEMS,)),
        ],
        input_output_aliases=alias,
        compiler_params=pltpu.CompilerParams(vmem_limit_bytes=16 << 20),
        cost_estimate=pl.CostEstimate(
            flops=4 * TOKENS * HALF * COLS // 4,
            bytes_accessed=6 << 20,
            transcendentals=0,
        ),
    )(lengths, mine, other, *pairs, *carried)


FAR = 2


def last_kernel(len_ref, scale_ref, mine_ref, other_ref, *refs):
    pairs, refs = (refs[0:2], refs[2:4]), refs[4:]
    moms, seq_a, seq_b, q_ins, refs = refs[0:2], refs[2:5], refs[5], refs[6:8], refs[8:]
    moments_ref, score_ref, w_ref, s_ref, q_ref, u_ref, g_ref, qg_ref, p_ref, out_ref, sem = refs
    y, _, _, _, c = where()
    copies = [
        group_copies(part, FAR, pairs[part], (mine_ref, other_ref), u_ref.at[part], g_ref.at[part], sem.at[part])
        for part in range(2)
    ]
    copies.append([pltpu.make_async_copy(ref.at[:, pl.ds(TOKENS, QROWS)], qg_ref.at[m], sem.at[2, m]) for m, ref in enumerate((mine_ref, other_ref))])
    for some in copies:
        for copy in (*some[2:], *some[:2]):
            copy.start()
    for part in range(2):
        w_ref[part] = moms[part][...]
        q_ref[part] = q_ins[part][...]
    for n, slot in enumerate((0, 1, 3)):
        s_ref[0, place(y, slot)] = seq_a[n][0]
    far = place(y, FAR)
    s_ref[0, far] = jnp.zeros((COLS, HALF), jnp.float32)
    s_ref[1] = seq_b[...]
    row = pl.multiple_of(far * 256, 256)
    seq_refs = s_ref.at[0, pl.ds(far, 1)], s_ref.at[1]
    q_refs = q_ref.at[0, pl.ds(row, 256), :], q_ref.at[1]
    for part in range(2):
        for copy in copies[part][2:]:
            copy.wait()
        for pair in range(2):
            copies[part][pair].wait()
            contract(part, FAR, pair, len_ref, u_ref.at[part], g_ref.at[part], w_ref.at[part], seq_refs[part], q_refs[part])
    for copy in copies[2]:
        copy.wait()

    mine_at = pl.multiple_of(c * BLOCK, BLOCK)
    other_at = pl.multiple_of((1 - c) * BLOCK, BLOCK)

    @pl.loop(0, FEAT // 256)
    def _(k):
        part, cols = k // 2, pl.ds(pl.multiple_of(lax.rem(k, 2) * 256, 256), 256)
        m = w_ref[part, :, cols] / scale_ref[SEQS]
        rows = pl.ds(pl.multiple_of(k * 256, 256), 256)
        out_ref[rows, pl.ds(mine_at, BLOCK)] = m[0:BLOCK, :].T
        out_ref[rows, pl.ds(other_at, BLOCK)] = m[BLOCK:COLS, :].T
        w_ref[part, :, cols] = 1.0 / (m + damping)

    leave = pltpu.make_async_copy(out_ref, moments_ref, sem.at[2, 2])
    leave.start()

    @pl.loop(0, SEQS)
    def _(s):
        for part in range(2):
            p = w_ref[part] * s_ref[part, s] * scale_ref[s]
            p_ref[part] = p.astype(jnp.bfloat16)

        @pl.loop(0, 2)
        def _(k):
            rows = pl.ds(pl.multiple_of(k * 512, 512), 512)
            mapped = dot(p_ref[0], q_ref[0, rows, :], 1, 1)
            mapped += dot(p_ref[1], q_ref[1, rows, :], 1, 1)
            total = jnp.sum(mapped[0:BLOCK] * qg_ref[0, :, rows].astype(jnp.float32), axis=0, keepdims=True)
            total += jnp.sum(mapped[BLOCK:COLS] * qg_ref[1, :, rows].astype(jnp.float32), axis=0, keepdims=True)
            score_ref[pl.ds(s, 1), rows] = total

    leave.wait()


def last(lengths, scales, mine, other, pairs, carried):
    return pl.pallas_call(
        last_kernel,
        out_shape=(
            jax.ShapeDtypeStruct((FEAT, COLS), jnp.float32),
            jax.ShapeDtypeStruct((SEQS, QROWS), jnp.float32),
        ),
        in_specs=[spec(SM)] * 2 + [spec(pltpu.HBM)] * 2 + [spec(ANY)] * 4 + [spec(VM)] * len(carried),
        out_specs=(spec(pltpu.HBM), spec(VM)),
        scratch_shapes=[
            pltpu.VMEM((2, COLS, HALF), jnp.float32),
            pltpu.VMEM((2, SEQS, COLS, HALF), jnp.float32),
            pltpu.VMEM((2, QROWS, HALF), jnp.bfloat16),
            pltpu.VMEM((2, HALVES, 2 * ROWS, HALF), jnp.bfloat16),
            pltpu.VMEM((2, 2, BLOCK, SEQ_LEN), jnp.bfloat16),
            pltpu.VMEM((2, BLOCK, QROWS), jnp.bfloat16),
            pltpu.VMEM((2, COLS, HALF), jnp.bfloat16),
            pltpu.VMEM((FEAT, COLS), jnp.float32),
            pltpu.SemaphoreType.DMA((3, SEMS)),
        ],
        compiler_params=pltpu.CompilerParams(vmem_limit_bytes=32 << 20),
        name="last",
    )(lengths, scales, mine, other, *pairs, *carried)


def shift(x, axis, step):
    return lax.ppermute(x, axis, [(i, (i + step) % RING) for i in range(RING)])


def spread(own, inner_axis, outer_axis, up):
    left = shift(own, inner_axis, 1)
    right = shift(own, inner_axis, -1)
    step, source = (1, left) if up else (-1, right)
    far = shift(source, inner_axis, step)
    pairs = (join(own, left), join(far, right))
    down = [shift(u, outer_axis, 1) for u in pairs]
    up = [shift(u, outer_axis, -1) for u in pairs]
    ends = (shift(down[0], outer_axis, 1), shift(up[1], outer_axis, -1))
    return [pairs, down, ends, up]


def at_z(k):
    k %= 2 * RING
    return k % RING * 2 + k // RING


def along_z(x, pairs):
    return lax.ppermute(x, (Z, H), [(at_z(a), at_z(b)) for a, b in pairs])


ONE = ((0, 1), (1, 2), (2, 3), (3, 4), (4, 7), (5, 0), (6, 5), (7, 6))
TWO = ((0, 5), (1, 6), (2, 7), (3, 0), (4, 3), (5, 4), (6, 1), (7, 2))
UP = tuple((k, k + 2) for k in range(8))
DOWN = tuple((k, k - 2) for k in range(8))


def local(act_in, grad_in, query_act, query_grad, act_basis, grad_basis, seq_lengths):
    own = rotate_act(seq_lengths, act_in, query_act, act_basis)
    blocks = [own] + [shift(own, Z, s) for s in range(1, RING)]

    packed = pack(grad_in, query_grad, own)
    received = lax.all_to_all(packed, (Y, X), 0, 0, tiled=True)
    odd, part = received[:, ROWS : 2 * ROWS], received[:, 2 * ROWS : SENT]
    parts = [received, along_z(odd, ONE), along_z(odd, TWO), along_z(part, UP), along_z(part, DOWN)]
    mine = rotate_grad(parts, grad_basis)
    other = lax.ppermute(mine, C, [(0, 1), (1, 0)])

    part_a, part_b = assemble(blocks)
    pairs = (spread(part_a, X, Y, True), spread(part_b, Y, X, False))
    moms, seqs, queries = [None, None], [[], []], [None, None]
    for outer in (0, 1, 3):
        for part in range(2):
            last_seqs = seqs[part][-1] if outer else None
            moms[part], s, queries[part] = group(part, outer, seq_lengths, mine, other, pairs[part][outer], moms[part], last_seqs, queries[part])
            seqs[part].append(s)

    counted = jnp.sum(seq_lengths).astype(jnp.float32)
    scales = jnp.concatenate(
        [lax.rsqrt(seq_lengths.astype(jnp.float32)), counted[None]]
    )
    carried = [*moms, *seqs[0], seqs[1][-1], *queries]
    far = [*pairs[0][FAR], *pairs[1][FAR]]
    moments, per_row = last(seq_lengths, scales, mine, other, far, carried)
    per_query = jnp.sum(per_row.reshape(SEQS, QUERIES, QUERY_LEN), axis=2)
    partial = per_query.reshape(2, 128) / math.sqrt(QUERY_LEN * D * FF)
    partial += lax.ppermute(partial, C, [(0, 1), (1, 0)])
    everywhere = jnp.broadcast_to(partial[None], (128, 2, 128))
    scores = lax.all_to_all(everywhere, (Y, X, Z, H), 0, 0, tiled=True).sum(0)
    return moments, scores.reshape(SEQS, QUERIES).T


def solution(mesh):
    finer = Mesh(mesh.devices.reshape(4, 4, 4, 2, 2), ALL)
    placed = (P(DP, MP), P(DP, None), P(DP, MP), P(DP, None), P(MP, None), P(DP, None), P())

    return jax.shard_map(
        local, mesh=finer, in_specs=placed, out_specs=(P(MP, DP), P()), check_vma=False
    )
```
